512 devices in a mesh: dp: 8 (over x, core), tm: 64 (over z, y).
Axes of the slice: x: 4, y: 8, z: 8, core: 2. Of those that a mesh axis runs over, the one named last changes fastest.
Arguments:
- samples: bfloat16 [8, 327680, 128], P('dp', 'tm'), may hold values from -6 to 6
- w_res: bfloat16 [3, 128, 64], replicated, may hold values from -0.3125 to 0.3125
- w_proj: bfloat16 [64, 128], replicated, may hold values from -0.75 to 0.75
- w_down: bfloat16 [10, 128, 256], replicated, may hold values from -0.15625 to 0.15625
- cotangent: bfloat16 [8, 65536, 256], P('dp', 'tm'), may hold values from -6 to 6
Outputs:
- encoded: bfloat16 [8, 65536, 256], P('dp', 'tm')
- d_input: bfloat16 [8, 327680, 128], P('dp', 'tm')
- grad_res: float32 [3, 128, 64], replicated
- grad_proj: float32 [64, 128], replicated
- grad_down: float32 [10, 128, 256], replicated
The draws below stay inside these ranges and needn't reach their ends.
All inputs are finite; a program needn't handle non-finite values.
Results may differ from the reference program's by a relative error of at most 0.0056.
Values may be sent and summed in bfloat16 or wider, within the bound.
No kernel may reach another device: no remote copies, remote signals or barrier semaphores. Data moves between devices by JAX's collectives and lax.ppermute only.
A program may use at most 64 MiB of HBM per device.

```python
import math
import jax
import jax.numpy as jnp
from jax import lax

C = 128
H = 64
CO = 256
STRIDE = 5
CLIPS = 8
FRAMES = 65536
SAMPLES = 327680


def levels(own_key, shape, shards, least, largest):
    def one(dim, blocks):
        draws = jax.random.uniform(jax.random.fold_in(jax.random.fold_in(own_key, 6), dim), (blocks,), jnp.float32, least / len(shards), largest / len(shards))
        return jnp.repeat(jnp.exp(draws), shape[dim] // blocks).reshape((-1,) + (1,) * (len(shape) - dim - 1))

    gain = one(*shards[0])
    for cut in shards[1:]:
        gain = gain * one(*cut)
    return gain


def bell_draw(key, dims, width, limit, shards=(), kind=jnp.bfloat16):
    gain = levels(key, dims, shards, -0.22, 0.18) if shards else 1.0
    result = jax.random.normal(key, dims, jnp.float32) * width * gain
    return jnp.minimum(jnp.maximum(result, -limit), limit).astype(kind)


def setup_inputs(seed: int = 0) -> dict:
    streams_of = jax.random.split(jax.random.key(seed), 6)
    return {
        "samples": bell_draw(streams_of[0], (CLIPS, SAMPLES, C), 1.0, 6.0, ((0, 8), (1, 64))),
        "w_res": bell_draw(streams_of[1], (3, C, H), (3 * C) ** -0.5, 0.3125),
        "w_proj": bell_draw(streams_of[2], (H, C), H ** -0.5, 0.75),
        "w_down": bell_draw(streams_of[3], (2 * STRIDE, C, CO), (2 * STRIDE * C) ** -0.5, 0.15625),
        "cotangent": bell_draw(streams_of[4], (CLIPS, FRAMES, CO), 1.0, 6.0, ((0, 8), (1, 64))),
    }


def elu_act(value):
    return jnp.where(value > 0, value, jnp.expm1(jnp.minimum(value, 0.0)))

def elu_slope(value):
    return jnp.where(value > 0, 1.0, jnp.exp(jnp.minimum(value, 0.0)))

def reference(samples, w_res, w_proj, w_down, cotangent):
    clip_count, length, channels = samples.shape
    frame_count = cotangent.shape[1]
    out_width = w_down.shape[2]
    hid_width = w_proj.shape[0]
    res_mat = w_res.reshape(3 * channels, hid_width)
    res_back = jnp.transpose(w_res, (0, 2, 1)).reshape(3 * hid_width, channels)
    down_lead = w_down[:STRIDE].reshape(STRIDE * channels, out_width)
    down_tail = w_down[STRIDE:].reshape(STRIDE * channels, out_width)

    def one_clip(carry, inputs):
        signal, grad_out = inputs
        signal_f = signal.astype(jnp.float32)
        activated = elu_act(signal_f).astype(jnp.bfloat16)
        act_pad = jnp.concatenate([jnp.zeros((2, channels), jnp.bfloat16), activated], axis=0)
        stacked = jnp.concatenate([act_pad[0:length], act_pad[1:length + 1], act_pad[2:length + 2]], axis=-1)
        hidden = jnp.dot(stacked, res_mat, preferred_element_type=jnp.float32)
        hidden_act = elu_act(hidden).astype(jnp.bfloat16)
        res_out = (signal_f + jnp.dot(hidden_act, w_proj, preferred_element_type=jnp.float32)).astype(jnp.bfloat16)
        squashed = elu_act(res_out.astype(jnp.float32)).astype(jnp.bfloat16)
        framed = jnp.concatenate([jnp.zeros((STRIDE, channels), jnp.bfloat16), squashed], axis=0)
        framed = framed.reshape(frame_count + 1, STRIDE * channels)
        encoded = (jnp.dot(framed[:-1], down_lead, preferred_element_type=jnp.float32) + jnp.dot(framed[1:], down_tail, preferred_element_type=jnp.float32)).astype(jnp.bfloat16)
        cot_ext = jnp.concatenate([grad_out, jnp.zeros((1, out_width), jnp.bfloat16)], axis=0)
        grad_sq = (jnp.dot(cot_ext[1:], down_lead.T, preferred_element_type=jnp.float32) + jnp.dot(cot_ext[:-1], down_tail.T, preferred_element_type=jnp.float32)).reshape(length, channels)
        grad_y = (grad_sq * elu_slope(res_out.astype(jnp.float32))).astype(jnp.bfloat16)
        grad_lead = jnp.dot(framed[:-1].T, grad_out, preferred_element_type=jnp.float32)
        grad_tail = jnp.dot(framed[1:].T, grad_out, preferred_element_type=jnp.float32)
        grad_pw = jnp.dot(hidden_act.T, grad_y, preferred_element_type=jnp.float32)
        grad_h = (jnp.dot(grad_y, w_proj.T, preferred_element_type=jnp.float32) * elu_slope(hidden)).astype(jnp.bfloat16)
        grad_first = jnp.dot(stacked.T, grad_h, preferred_element_type=jnp.float32)
        hidden_ext = jnp.concatenate([grad_h, jnp.zeros((2, hid_width), jnp.bfloat16)], axis=0)
        pieces = jnp.concatenate([hidden_ext[2:length + 2], hidden_ext[1:length + 1], hidden_ext[0:length]], axis=-1)
        grad_act = jnp.dot(pieces, res_back, preferred_element_type=jnp.float32)
        d_input = (grad_y.astype(jnp.float32) + grad_act * elu_slope(signal_f)).astype(jnp.bfloat16)
        carry = (carry[0] + grad_first, carry[1] + grad_pw, carry[2] + grad_lead, carry[3] + grad_tail)
        return (carry, (encoded, d_input))
    start = (jnp.zeros((3 * channels, hid_width), jnp.float32), jnp.zeros((hid_width, channels), jnp.float32), jnp.zeros((STRIDE * channels, out_width), jnp.float32), jnp.zeros((STRIDE * channels, out_width), jnp.float32))
    sums, outputs = lax.scan(one_clip, start, (samples, cotangent))
    scale = 1.0 / math.sqrt(clip_count * frame_count)
    grad_res = (sums[0] * scale).reshape(3, channels, hid_width)
    grad_proj = sums[1] * scale
    grad_down = jnp.concatenate([sums[2].reshape(STRIDE, channels, out_width), sums[3].reshape(STRIDE, channels, out_width)], axis=0) * scale
    return (outputs[0], outputs[1], grad_res, grad_proj, grad_down)
```

```python
import math

import jax
import jax.numpy as jnp
from jax import lax
from jax.sharding import Mesh, PartitionSpec as P

STRIDE = 5


X, CORE, Z, Y = 4, 2, 8, 8
XC = X * CORE
LANES = 128
TM = ("z", "y")


def exchange(blocks, axes):
    return lax.all_to_all(blocks, axes, 0, 0, tiled=True)


def scatter_sum(value, axes, count):
    blocks = value.astype(jnp.bfloat16).reshape(count, value.shape[0] // count, LANES)
    return jnp.sum(exchange(blocks, axes).astype(jnp.float32), axis=0)


def copies(value, axes, count):
    return exchange(jnp.broadcast_to(value[None], (count,) + value.shape), axes)


def total(value):
    part = scatter_sum(value, ("x", "core"), XC)
    part = scatter_sum(part, "y", Y)
    part = jnp.sum(copies(part.astype(jnp.bfloat16), "z", Z).astype(jnp.float32), axis=0)
    part = part.astype(jnp.bfloat16)
    part = copies(part, "y", Y).reshape(-1, LANES)
    return copies(part, ("x", "core"), XC).reshape(-1, LANES)


def from_behind(value, axis, steps):
    count = lax.axis_size(axis)
    first, last = (max(0, -steps), min(count, count - steps))
    return lax.ppermute(value, axis, [(source, source + steps) for source in range(first, last)])


def elu_act(value):
    return jnp.where(value > 0, value, jnp.expm1(jnp.minimum(value, 0.0)))


def elu_slope(value):
    return jnp.where(value > 0, 1.0, jnp.exp(jnp.minimum(value, 0.0)))


def residual_unit(extended, w_res, w_proj):
    length = extended.shape[1] - 2
    channels = extended.shape[2]
    activated = elu_act(extended.astype(jnp.float32)).astype(jnp.bfloat16)
    stacked = jnp.concatenate(
        [activated[:, 0:length], activated[:, 1 : length + 1], activated[:, 2 : length + 2]],
        axis=-1,
    )
    res_mat = w_res.reshape(3 * channels, w_res.shape[2])
    hidden = jnp.einsum("ntk,kh->nth", stacked, res_mat, preferred_element_type=jnp.float32)
    hidden_act = elu_act(hidden).astype(jnp.bfloat16)
    branch = jnp.einsum("nth,hc->ntc", hidden_act, w_proj, preferred_element_type=jnp.float32)
    res_out = (extended[:, 2:].astype(jnp.float32) + branch).astype(jnp.bfloat16)
    return (stacked, hidden, hidden_act, res_out)


def shards(samples, w_res, w_proj, w_down, cotangent):
    clip_count = samples.shape[0]
    length = samples.shape[1]
    channels = samples.shape[2]
    frame_count = cotangent.shape[1]
    out_width = w_down.shape[2]
    hid_width = w_proj.shape[0]
    rim_rows = from_behind(samples[:, length - 2 :], TM, 1)
    extended = jnp.concatenate([rim_rows, samples], axis=1)
    stacked, hidden, hidden_act, res_own = residual_unit(extended, w_res, w_proj)
    res_rim = from_behind(res_own[:, length - STRIDE :], TM, 1)
    res_ext = jnp.concatenate([res_rim, res_own], axis=1)
    squashed = elu_act(res_ext.astype(jnp.float32)).astype(jnp.bfloat16)
    framed = squashed.reshape(clip_count, frame_count + 1, STRIDE * channels)
    down_lead = w_down[:STRIDE].reshape(STRIDE * channels, out_width)
    down_tail = w_down[STRIDE:].reshape(STRIDE * channels, out_width)
    encoded = (
        jnp.einsum("nsk,ko->nso", framed[:, :-1], down_lead, preferred_element_type=jnp.float32)
        + jnp.einsum("nsk,ko->nso", framed[:, 1:], down_tail, preferred_element_type=jnp.float32)
    ).astype(jnp.bfloat16)
    next_row = from_behind(cotangent[:, :1], TM, -1)
    cot_ext = jnp.concatenate([cotangent, next_row], axis=1)
    grad_sq = jnp.einsum(
        "nso,ko->nsk", cot_ext[:, 1:], down_lead, preferred_element_type=jnp.float32
    ) + jnp.einsum("nso,ko->nsk", cot_ext[:, :-1], down_tail, preferred_element_type=jnp.float32)
    grad_sq = grad_sq.reshape(clip_count, length, channels)
    grad_y = (grad_sq * elu_slope(res_own.astype(jnp.float32))).astype(jnp.bfloat16)
    grad_lead = jnp.einsum(
        "nsk,nso->ko", framed[:, :-1], cotangent, preferred_element_type=jnp.float32
    )
    grad_tail = jnp.einsum(
        "nsk,nso->ko", framed[:, 1:], cotangent, preferred_element_type=jnp.float32
    )
    grad_pw = jnp.einsum("nth,ntc->hc", hidden_act, grad_y, preferred_element_type=jnp.float32)
    grad_h = (
        jnp.einsum("ntc,hc->nth", grad_y, w_proj, preferred_element_type=jnp.float32)
        * elu_slope(hidden)
    ).astype(jnp.bfloat16)
    grad_first = jnp.einsum("ntk,nth->kh", stacked, grad_h, preferred_element_type=jnp.float32)
    hidden_next = from_behind(grad_h[:, :2], TM, -1)
    hidden_ext = jnp.concatenate([grad_h, hidden_next], axis=1)
    pieces = jnp.concatenate(
        [hidden_ext[:, 2 : length + 2], hidden_ext[:, 1 : length + 1], hidden_ext[:, 0:length]],
        axis=-1,
    )
    res_back = jnp.transpose(w_res, (0, 2, 1)).reshape(3 * hid_width, channels)
    grad_act = jnp.einsum("ntk,kc->ntc", pieces, res_back, preferred_element_type=jnp.float32)
    d_input = (
        grad_y.astype(jnp.float32) + grad_act * elu_slope(samples.astype(jnp.float32))
    ).astype(jnp.bfloat16)
    flat = jnp.concatenate(
        [grad_first.reshape(-1), grad_pw.reshape(-1), grad_lead.reshape(-1), grad_tail.reshape(-1)]
    )
    size = flat.shape[0]
    rows = -(-size // (LANES * XC * Y * 16)) * XC * Y * 16
    flat = jnp.pad(flat, (0, rows * LANES - size)).reshape(rows, LANES)
    scale = 1.0 / math.sqrt(clip_count * XC * frame_count * Y * Z)
    summed = total(flat * scale).astype(jnp.float32).reshape(-1)[:size]
    first_end = 3 * channels * hid_width
    proj_end = first_end + hid_width * channels
    lead_end = proj_end + STRIDE * channels * out_width
    grad_res = summed[:first_end].reshape(3, channels, hid_width)
    grad_proj = summed[first_end:proj_end].reshape(hid_width, channels)
    grad_down = jnp.concatenate(
        [
            summed[proj_end:lead_end].reshape(STRIDE, channels, out_width),
            summed[lead_end:].reshape(STRIDE, channels, out_width),
        ],
        axis=0,
    )
    return (encoded, d_input, grad_res, grad_proj, grad_down)


def solution(mesh):
    mesh = Mesh(mesh.devices.reshape(X, CORE, Z, Y), ("x", "core", "z", "y"))
    data = P(("x", "core"), TM, None)
    in_specs = (data, P(), P(), P(), data)
    out_specs = (data, data, P(), P(), P())
    return jax.shard_map(shards, mesh=mesh, in_specs=in_specs, out_specs=out_specs, check_vma=False)
```

```python
import functools
import math

import jax
import jax.numpy as jnp
from jax import lax
from jax.experimental import pallas as pl
from jax.experimental.pallas import tpu as pltpu
from jax.sharding import Mesh, PartitionSpec as P

STRIDE = 5
X, CORE, Z, Y = 4, 2, 8, 8
XC = X * CORE
LANES = 128
EDGE = 16
BLOCK = 256
LIMIT = 20 * 2**20
MOST = 62_500_000
TM = ("z", "y")
BF = jnp.bfloat16
F32 = jnp.float32
VMEM = pl.BlockSpec(memory_space=pltpu.VMEM)
ANY = pl.BlockSpec(memory_space=pltpu.HBM)


def shape(rows, columns, kind=BF):
    return jax.ShapeDtypeStruct((rows, columns), kind)


def from_behind(value, steps):
    count = Z * Y
    first, last = (max(0, -steps), min(count, count - steps))
    return lax.ppermute(value, TM, [(source, source + steps) for source in range(first, last)])


def exchange(blocks, axes):
    return lax.all_to_all(blocks, axes, 0, 0, tiled=True)


def scatter_sum(value, axes, count):
    blocks = value.astype(BF).reshape(count, value.shape[0] // count, LANES)
    return jnp.sum(exchange(blocks, axes).astype(F32), axis=0)


def copies(value, axes, count):
    return exchange(jnp.broadcast_to(value[None], (count,) + value.shape), axes)


def total(value):
    part = scatter_sum(value, ("x", "core"), XC)
    part = scatter_sum(part, "y", Y)
    part = jnp.sum(copies(part.astype(BF), "z", Z).astype(F32), axis=0)
    part = part.astype(BF)
    part = copies(part, "y", Y).reshape(-1, LANES)
    return copies(part, ("x", "core"), XC).reshape(-1, LANES)


def dot(a, b):
    return jnp.dot(a, b, preferred_element_type=F32)


def dot_rows(a, b):
    return lax.dot_general(a, b, (((0,), (0,)), ((), ())), preferred_element_type=F32)


def dot_lanes(a, b):
    return lax.dot_general(a, b, (((1,), (1,)), ((), ())), preferred_element_type=F32)


def slope_of(v):
    return jnp.exp(jnp.minimum(v, 0.0))


def elu_of(v, slope):
    return jnp.maximum(v, 0.0) + (slope - 1.0)


def elu(v):
    return elu_of(v, slope_of(v))


def lanes(*pieces):
    return jnp.concatenate(pieces, axis=1)


def frames(xs, acts, before, cot, cot_next, w_conv, w_pair, w_lead, w_tail):
    inputs = (
        lanes(before[0], before[1], acts[0], acts[1]),
        lanes(acts[0], acts[1], acts[2], acts[3]),
        lanes(acts[2], acts[3], acts[4]),
    )
    grad_sq = dot_lanes(cot_next, w_lead) + dot_lanes(cot, w_tail)
    squashed, grad_y, grad_h, hidden_act = [], [], [], []
    for pair, stacked in enumerate(inputs):
        wide = 2 if pair < 2 else 1
        hidden = dot_lanes(stacked, w_conv[:, : stacked.shape[1]])
        if wide == 1:
            hidden = jnp.where(lax.broadcasted_iota(jnp.int32, hidden.shape, 1) < LANES // 2, hidden, 0.0)
        slope_h = slope_of(hidden)
        act_h = elu_of(hidden, slope_h).astype(BF)
        branch = dot(act_h, w_pair[:, : wide * LANES])
        own = []
        for k in range(wide):
            p = 2 * pair + k
            res = (xs[p] + branch[:, k * LANES : (k + 1) * LANES]).astype(BF).astype(F32)
            slope_r = slope_of(res)
            squashed.append(elu_of(res, slope_r).astype(BF))
            own.append((grad_sq[:, p * LANES : (p + 1) * LANES] * slope_r).astype(BF))
        own = own[0] if wide == 1 else lanes(*own)
        grad_y.append(own)
        grad_h.append((dot_lanes(own, w_pair[:, : wide * LANES]) * slope_h).astype(BF))
        hidden_act.append(act_h)
    return inputs, squashed, grad_y, grad_h, hidden_act


def pair_weights(w_res, w_proj):
    zero = jnp.zeros_like(w_res[0])
    w_conv = jnp.concatenate([lanes(w_res[0], w_res[1], w_res[2], zero), lanes(zero, w_res[0], w_res[1], w_res[2])], axis=0)
    none = jnp.zeros_like(w_proj)
    w_pair = jnp.concatenate([lanes(w_proj, none), lanes(none, w_proj)], axis=0)
    return w_conv, w_pair


def rim_kernel(x_hbm, cot_hbm, tail_ref, head_ref, sem):
    size = tail_ref.shape[0]
    moves = (
        (x_hbm.at[pl.ds(x_hbm.shape[0] - size, size)], tail_ref),
        (x_hbm.at[pl.ds(0, size)], head_ref.at[:, pl.ds(0, LANES)]),
        (cot_hbm.at[pl.ds(0, size)], head_ref.at[:, pl.ds(LANES, 2 * LANES)]),
    )
    moves = [pltpu.make_async_copy(source, target, sem.at[k]) for k, (source, target) in enumerate(moves)]
    for move in moves:
        move.start()
    for move in moves:
        move.wait()


def first_kernel(
    scale, x_hbm, cot_hbm, behind_ref, ahead_ref, res_ref, proj_ref, down_hbm,
    sq_hbm, gy_hbm, gh_hbm, esq_ref, egh_ref, pack_ref,
    x_ref, cot_ref, down_ref, sq_ref, gy_ref, gh_ref, xf, act3, act4, cotf, acc_down, acc_res, acc_proj, conv_ref, pair_ref,
    in_sem, x_sem, out_sem,
):
    length, count = x_ref.shape[0], cot_ref.shape[0]
    taps = STRIDE * LANES
    steps = count // BLOCK
    load_cot = pltpu.make_async_copy(cot_hbm, cot_ref, in_sem.at[0])
    load_down = pltpu.make_async_copy(down_hbm, down_ref, in_sem.at[1])
    load_cot.start()
    load_down.start()

    def load_x(i):
        rows = pl.ds(pl.multiple_of(i * STRIDE * BLOCK, STRIDE * BLOCK), STRIDE * BLOCK)
        return pltpu.make_async_copy(x_hbm.at[rows], x_ref.at[rows], x_sem.at[i])

    def store(i, k):
        rows = pl.ds(pl.multiple_of(i * BLOCK, BLOCK), BLOCK)
        here, there = ((sq_ref, sq_hbm), (gy_ref, gy_hbm), (gh_ref, gh_hbm))[k]
        return pltpu.make_async_copy(here.at[rows], there.at[rows], out_sem.at[k, i])

    for i in range(steps):
        load_x(i).start()
    conv_ref[...], pair_ref[...] = pair_weights(res_ref[...], proj_ref[...])
    load_cot.wait()
    for k in range(2):
        cotf[k, pl.ds(0, count)] = cot_ref[:, k * LANES : (k + 1) * LANES].astype(F32)
    behind = behind_ref[...].astype(F32)
    ahead = ahead_ref[:, :LANES].astype(F32)
    cot_ahead = [ahead_ref[:, k * LANES : (k + 1) * LANES].astype(F32) for k in (1, 2)]
    for k in range(2):
        cotf[k, pl.ds(count, 8)] = jnp.broadcast_to(cot_ahead[k][0:1], (8, LANES))
    act3[pl.ds(0, 8)] = jnp.broadcast_to(elu(behind[14:15]), (8, LANES))
    act4[pl.ds(0, 8)] = jnp.broadcast_to(elu(behind[15:16]), (8, LANES))
    acc_down[...] = jnp.zeros_like(acc_down)
    acc_res[...] = jnp.zeros_like(acc_res)
    acc_proj[...] = jnp.zeros_like(acc_proj)
    w_lead, w_tail = down_ref.at[pl.ds(0, taps)], down_ref.at[pl.ds(taps, taps)]
    load_down.wait()

    def block(i, _):
        r = pl.multiple_of(i * BLOCK, BLOCK)
        rows = pl.ds(r, BLOCK)
        load_x(i).wait()
        some = pl.ds(pl.multiple_of(STRIDE * r, STRIDE * BLOCK), STRIDE * BLOCK)
        xf[some] = x_ref[some].astype(F32)
        xs = [xf[pl.ds(STRIDE * r + p, BLOCK, stride=STRIDE)] for p in range(STRIDE)]
        acts = [elu(x) for x in xs]
        act3[pl.ds(r + 8, BLOCK)] = acts[3]
        act4[pl.ds(r + 8, BLOCK)] = acts[4]
        acts = [a.astype(BF) for a in acts]
        before = [a[pl.ds(r + 7, BLOCK)].astype(BF) for a in (act3, act4)]
        cot = cot_ref[rows]
        cot_next = lanes(*[cotf[k, pl.ds(r + 1, BLOCK)].astype(BF) for k in range(2)])
        inputs, squashed, grad_y, grad_h, hidden_act = frames(
            xs, acts, before, cot, cot_next, conv_ref[...], pair_ref[...], w_lead[...], w_tail[...]
        )
        squashed = lanes(*squashed)
        sq_ref[rows] = squashed
        gy_ref[rows] = lanes(*grad_y)
        gh_ref[rows] = lanes(*grad_h)
        acc_down[...] += dot_rows(squashed, lanes(cot_next, cot))
        for k in range(3):
            n, m = inputs[k].shape[1], grad_y[k].shape[1]
            acc_res[:, :n] += dot_rows(grad_h[k], inputs[k])
            acc_proj[:, :m] += dot_rows(hidden_act[k], grad_y[k])
        for k in range(3):
            store(i, k).start()
        return 0

    lax.fori_loop(0, steps, block, 0)

    def edge(first, second):
        return jnp.concatenate([first, second, jnp.zeros((EDGE - 2, LANES), F32)], axis=0)

    last = [act[pl.ds(count, 8)][7:8] for act in (act3, act4)]
    blank = jnp.zeros((1, LANES), F32)
    xs = [edge(behind[11 + p : 12 + p], ahead[p : p + 1] if p < 2 else blank) for p in range(STRIDE)]
    before = [edge(elu(behind[9 + k : 10 + k]), last[k]).astype(BF) for k in range(2)]
    cot = lanes(*[edge(blank, cot_ahead[k][0:1]) for k in range(2)]).astype(BF)
    cot_next = lanes(*[edge(blank, cot_ahead[k][1:2]) for k in range(2)]).astype(BF)
    _, squashed, _, grad_h, _ = frames(
        xs, [elu(x).astype(BF) for x in xs], before, cot, cot_next, conv_ref[...], pair_ref[...], w_lead[...], w_tail[...]
    )
    esq_ref[...] = lanes(*squashed)
    egh_ref[...] = grad_h[0]

    for k in range(4):
        pack_ref[pl.ds(k * taps, taps)] = (acc_down[:, k * LANES : (k + 1) * LANES] * scale).astype(BF)
    half = LANES // 2
    at = 4 * taps
    for j in range(3):
        block_j = acc_res[:half, j * LANES : (j + 1) * LANES] + acc_res[half:, (j + 1) * LANES : (j + 2) * LANES]
        pack_ref[pl.ds(at + j * half, half)] = (block_j * scale).astype(BF)
    block_j = acc_proj[:half, :LANES] + acc_proj[half:, LANES:]
    at += 3 * half
    pack_ref[pl.ds(at, half)] = (block_j * scale).astype(BF)
    at += half
    pack_ref[pl.ds(at, pack_ref.shape[0] - at)] = jnp.zeros((pack_ref.shape[0] - at, LANES), BF)
    for i in range(steps):
        for k in range(3):
            store(i, k).wait()


def second_kernel(
    x_ref, sq_ref, gy_ref, gh_ref, esq_ref, egh_ref, res_ref, down_ref, enc_ref, out_ref, xf, gf, lead, mix_ref,
):
    length, count = x_ref.shape[0], sq_ref.shape[0]
    taps = STRIDE * LANES
    w = [res_ref[j] for j in range(3)]
    zero = jnp.zeros_like(w[0])
    mix_ref[...] = jnp.concatenate(
        [
            lanes(w[2], zero, zero), lanes(w[1], w[2], zero), lanes(w[0], w[1], w[2]), lanes(zero, w[0], w[1]),
            lanes(zero, w[0], w[1]), lanes(zero, zero, w[0]),
        ],
        axis=0,
    )

    def widen(i, _):
        r = pl.multiple_of(i * BLOCK, BLOCK)
        xf[pl.ds(r, BLOCK)] = x_ref[pl.ds(r, BLOCK)].astype(F32)
        return 0

    lax.fori_loop(0, length // BLOCK, widen, 0)
    gf[pl.ds(0, count)] = gh_ref[:, :LANES].astype(F32)
    gf[pl.ds(count, 8)] = jnp.broadcast_to(egh_ref[...].astype(F32)[1:2], (8, LANES))
    w_lead, w_tail = down_ref.at[pl.ds(0, taps)], down_ref.at[pl.ds(taps, taps)]
    start = dot(esq_ref[...], w_lead[...])
    for k in range(2):
        lead[k, pl.ds(0, 8)] = jnp.broadcast_to(start[0:1, k * LANES : (k + 1) * LANES], (8, LANES))

    def block(i, _):
        r = pl.multiple_of(i * BLOCK, BLOCK)
        rows = pl.ds(r, BLOCK)
        squashed = sq_ref[rows]
        first = dot(squashed, w_lead[...])
        for k in range(2):
            lead[k, pl.ds(r + 8, BLOCK)] = first[:, k * LANES : (k + 1) * LANES]
        shifted = lanes(*[lead[k, pl.ds(r + 7, BLOCK)] for k in range(2)])
        enc_ref[rows] = (shifted + dot(squashed, w_tail[...])).astype(BF)
        grad_h = gh_ref[rows]
        later = gf[pl.ds(r + 1, BLOCK)].astype(BF)
        grad_a = lanes(
            dot(grad_h[:, : 2 * LANES], mix_ref[: 2 * LANES, : 2 * LANES]),
            dot(lanes(grad_h[:, LANES:], later), mix_ref[...]),
        )
        for p in range(STRIDE):
            here = pl.ds(STRIDE * r + p, BLOCK, stride=STRIDE)
            own = slice(p * LANES, (p + 1) * LANES)
            xf[here] = gy_ref[rows, own].astype(F32) + grad_a[:, own] * slope_of(xf[here])
        return 0

    lax.fori_loop(0, count // BLOCK, block, 0)

    def narrow(i, _):
        r = pl.multiple_of(i * BLOCK, BLOCK)
        out_ref[pl.ds(r, BLOCK)] = xf[pl.ds(r, BLOCK)].astype(BF)
        return 0

    lax.fori_loop(0, length // BLOCK, narrow, 0)


def last_kernel(pack_ref, res_ref, proj_ref, down_ref):
    taps, half = STRIDE * LANES, LANES // 2
    for k in range(4):
        for p in range(STRIDE):
            block = pack_ref[pl.ds(k * taps + p * LANES, LANES)].astype(F32)
            down_ref[STRIDE * (k // 2) + p, :, pl.ds((k % 2) * LANES, LANES)] = block
    at = 4 * taps
    for j in range(3):
        res_ref[j] = pack_ref[pl.ds(at + j * half, half)].astype(F32)
    proj_ref[...] = pack_ref[pl.ds(at + 3 * half, half)].astype(F32)


def shards(samples, w_res, w_proj, w_down, cotangent):
    clip_count, length, channels = samples.shape
    frame_count, out_width = cotangent.shape[1:]
    hid_width = w_proj.shape[0]
    taps = STRIDE * channels
    x, cot = samples[0], cotangent[0]
    down = w_down.reshape(2 * taps, out_width)
    w_res = jnp.transpose(w_res, (0, 2, 1))
    tail, head = pl.pallas_call(
        rim_kernel,
        out_shape=(shape(EDGE, LANES), shape(EDGE, 3 * LANES)),
        in_specs=[ANY] * 2,
        out_specs=(VMEM,) * 2,
        scratch_shapes=[pltpu.SemaphoreType.DMA((3,))],
        compiler_params=pltpu.CompilerParams(vmem_limit_bytes=MOST),
        name="rim",
    )(x, cot)
    behind, ahead = from_behind(tail, 1), from_behind(head, -1)
    size = 2 * taps * out_width + 3 * channels * hid_width + hid_width * channels
    rows = -(-size // (LANES * XC * Y * 16)) * XC * Y * 16
    scale = 1.0 / math.sqrt(clip_count * XC * frame_count * Y * Z)
    squashed, grad_y, grad_h, edge_sq, edge_gh, pack = pl.pallas_call(
        functools.partial(first_kernel, scale),
        out_shape=(
            shape(frame_count, taps), shape(frame_count, taps), shape(frame_count, 3 * LANES),
            shape(EDGE, taps), shape(EDGE, LANES), shape(rows, LANES),
        ),
        in_specs=[ANY, ANY, VMEM, VMEM, VMEM, VMEM, ANY],
        out_specs=(ANY, ANY, ANY, VMEM, VMEM, VMEM),
        scratch_shapes=[
            pltpu.VMEM((length, LANES), BF),
            pltpu.VMEM((frame_count, out_width), BF),
            pltpu.VMEM((2 * taps, out_width), BF),
            pltpu.VMEM((frame_count, taps), BF),
            pltpu.VMEM((frame_count, taps), BF),
            pltpu.VMEM((frame_count, 3 * LANES), BF),
            pltpu.VMEM((length, LANES), F32),
            pltpu.VMEM((frame_count + 8, LANES), F32),
            pltpu.VMEM((frame_count + 8, LANES), F32),
            pltpu.VMEM((2, frame_count + 8, LANES), F32),
            pltpu.VMEM((taps, 2 * out_width), F32),
            pltpu.VMEM((LANES, 4 * LANES), F32),
            pltpu.VMEM((LANES, 2 * LANES), F32),
            pltpu.VMEM((LANES, 4 * LANES), BF),
            pltpu.VMEM((LANES, 2 * LANES), BF),
            pltpu.SemaphoreType.DMA((2,)),
            pltpu.SemaphoreType.DMA((frame_count // BLOCK,)),
            pltpu.SemaphoreType.DMA((3, frame_count // BLOCK)),
        ],
        compiler_params=pltpu.CompilerParams(vmem_limit_bytes=MOST),
        cost_estimate=pl.CostEstimate(flops=3 * 10**9, bytes_accessed=6 * 10**6, transcendentals=2 * 10**6),
        name="first",
    )(x, cot, behind, ahead, w_res, w_proj, down)
    encoded, d_input = pl.pallas_call(
        second_kernel,
        out_shape=(shape(frame_count, out_width), shape(length, channels)),
        in_specs=[VMEM] * 8,
        out_specs=(VMEM,) * 2,
        scratch_shapes=[
            pltpu.VMEM((length, LANES), F32),
            pltpu.VMEM((frame_count + 8, LANES), F32),
            pltpu.VMEM((2, frame_count + 8, LANES), F32),
            pltpu.VMEM((3 * LANES, 3 * LANES), BF),
        ],
        compiler_params=pltpu.CompilerParams(vmem_limit_bytes=LIMIT),
        cost_estimate=pl.CostEstimate(flops=2 * 10**9, bytes_accessed=8 * 10**6, transcendentals=10**6),
        name="second",
    )(x, squashed, grad_y, grad_h, edge_sq, edge_gh, w_res, down)
    summed = total(pack)
    grad_res, grad_proj, grad_down = pl.pallas_call(
        last_kernel,
        out_shape=(
            jax.ShapeDtypeStruct((3, hid_width, channels), F32),
            jax.ShapeDtypeStruct((hid_width, channels), F32),
            jax.ShapeDtypeStruct((2 * STRIDE, channels, out_width), F32),
        ),
        in_specs=[VMEM],
        out_specs=(VMEM,) * 3,
        compiler_params=pltpu.CompilerParams(vmem_limit_bytes=LIMIT),
        name="last",
    )(summed)
    return (encoded[None], d_input[None], jnp.transpose(grad_res, (0, 2, 1)), grad_proj, grad_down)


def solution(mesh):
    mesh = Mesh(mesh.devices.reshape(X, CORE, Z, Y), ("x", "core", "z", "y"))
    data = P(("x", "core"), TM, None)
    in_specs = (data, P(), P(), P(), data)
    out_specs = (data, data, P(), P(), P())
    return jax.shard_map(shards, mesh=mesh, in_specs=in_specs, out_specs=out_specs, check_vma=False)
```

```python
import functools
import math

import jax
import jax.numpy as jnp
from jax import lax
from jax.experimental import pallas as pl
from jax.experimental.pallas import tpu as pltpu
from jax.sharding import Mesh, PartitionSpec as P

STRIDE = 5
X, CORE, Z, Y = 4, 2, 8, 8
XC = X * CORE
LANES = 128
EDGE = 16
BLOCK = 1024
LIMIT = 32 * 2**20
TM = ("z", "y")
BF = jnp.bfloat16
F32 = jnp.float32
VMEM = pl.BlockSpec(memory_space=pltpu.VMEM)
ANY = pl.BlockSpec(memory_space=pltpu.HBM)


def shape(rows, columns, kind=BF):
    return jax.ShapeDtypeStruct((rows, columns), kind)


def from_behind(value, steps):
    count = Z * Y
    first, last = (max(0, -steps), min(count, count - steps))
    return lax.ppermute(value, TM, [(source, source + steps) for source in range(first, last)])


def exchange(blocks, axes):
    return lax.all_to_all(blocks, axes, 0, 0, tiled=True)


def copies(value, axes, count):
    return exchange(jnp.broadcast_to(value[None], (count,) + value.shape), axes)


def swap(value):
    return lax.ppermute(value, "core", [(0, 1), (1, 0)])


def total(mine, other, beside):
    part = (mine.astype(F32) + swap(other).astype(F32)).astype(BF)
    part = jnp.sum(exchange(part.reshape(X * Y, -1, LANES), ("x", "y")).astype(F32), axis=0).astype(BF)
    part = jnp.sum(copies(part, "z", Z).astype(F32), axis=0).astype(BF)
    part, gate = lax.optimization_barrier((part, beside[0]))
    outputs = second_call(gate, *beside[1:])
    part = copies(part, ("x", "y"), X * Y).reshape(-1, LANES)
    part, *outputs = lax.optimization_barrier((part, *outputs))
    return part, swap(part), outputs


def dot(a, b):
    return jnp.dot(a, b, preferred_element_type=F32)


def dot_rows(a, b):
    return lax.dot_general(a, b, (((0,), (0,)), ((), ())), preferred_element_type=F32)


def slope_of(v):
    return jnp.exp(jnp.minimum(v, 0.0))


def elu_of(v, slope):
    return jnp.maximum(v, 0.0) + (slope - 1.0)


def elu(v):
    return elu_of(v, slope_of(v))


def lanes(*pieces):
    return jnp.concatenate(pieces, axis=1)


def rim_kernel(x_hbm, cot_hbm, tail_ref, head_ref, sem):
    size, end, last = EDGE, x_hbm.shape[0] - EDGE, cot_hbm.shape[0] - EDGE
    moves = (
        (x_hbm.at[pl.ds(end, size)], tail_ref.at[:, pl.ds(0, LANES)]),
        (cot_hbm.at[pl.ds(last, size)], tail_ref.at[:, pl.ds(LANES, 2 * LANES)]),
        (x_hbm.at[pl.ds(0, size)], head_ref.at[:, pl.ds(0, LANES)]),
        (cot_hbm.at[pl.ds(0, size)], head_ref.at[:, pl.ds(LANES, 2 * LANES)]),
    )
    moves = [pltpu.make_async_copy(source, target, sem.at[k]) for k, (source, target) in enumerate(moves)]
    for move in moves:
        move.start()
    for move in moves:
        move.wait()


def frames(xs, acts, before, cots, weights):
    w_conv, w_pair, w_back, w_grad = [w[...] for w in weights]
    inputs = (
        lanes(before[0], before[1], acts[0], acts[1]),
        lanes(acts[0], acts[1], acts[2], acts[3]),
        lanes(acts[2], acts[3], acts[4]),
    )
    grad_sq = dot(cots, w_grad)
    squashed, grad_y, grad_h, hidden_act = [], [], [], []
    for pair, stacked in enumerate(inputs):
        wide = 2 if pair < 2 else 1
        hidden = dot(stacked, w_conv[: stacked.shape[1]])
        if wide == 1:
            hidden = jnp.where(lax.broadcasted_iota(jnp.int32, hidden.shape, 1) < LANES // 2, hidden, 0.0)
        slope_h = slope_of(hidden)
        act_h = elu_of(hidden, slope_h).astype(BF)
        branch = dot(act_h, w_pair[:, : wide * LANES])
        own = []
        for k in range(wide):
            p = 2 * pair + k
            res = (xs[p] + branch[:, k * LANES : (k + 1) * LANES]).astype(BF).astype(F32)
            slope_r = slope_of(res)
            squashed.append(elu_of(res, slope_r).astype(BF))
            own.append((grad_sq[:, p * LANES : (p + 1) * LANES] * slope_r).astype(BF))
        own = own[0] if wide == 1 else lanes(*own)
        grad_y.append(own)
        grad_h.append((dot(own, w_back[: wide * LANES]) * slope_h).astype(BF))
        hidden_act.append(act_h)
    return inputs, squashed, grad_y, grad_h, hidden_act


def prepare(res_ref, proj_ref, down_ref, weights):
    w_conv, w_pair, w_back, w_grad = weights
    taps = STRIDE * LANES
    w = [res_ref[j] for j in range(3)]
    zero = jnp.zeros_like(w[0])
    above = (*w, zero)
    below = (zero, *w)
    for k in range(4):
        block = jnp.concatenate([above[k], below[k]], axis=0)
        w_conv[pl.ds(k * LANES, LANES)] = jnp.transpose(block)
    proj = proj_ref[...]
    none = jnp.zeros_like(proj)
    for k in range(2):
        block = jnp.concatenate([none, proj] if k else [proj, none], axis=0)
        w_pair[:, pl.ds(k * LANES, LANES)] = block
        w_back[pl.ds(k * LANES, LANES)] = jnp.transpose(block)
    for part in range(2):
        for p in range(STRIDE):
            for k in range(2):
                block = down_ref[pl.ds(part * taps + p * LANES, LANES), pl.ds(k * LANES, LANES)]
                w_grad[pl.ds((2 * part + k) * LANES, LANES), pl.ds(p * LANES, LANES)] = jnp.transpose(block)


def shift_cot(cot_ref, cotf, last):
    count = cot_ref.shape[0]
    for k in range(2):
        cotf[k, pl.ds(0, count)] = cot_ref[:, k * LANES : (k + 1) * LANES].astype(F32)
        cotf[k, pl.ds(count, 8)] = jnp.broadcast_to(last[k], (8, LANES))


def pre_kernel(x_ref, cot_ref, res_ref, proj_ref, down_ref, phase_ref, next_ref, w0_ref, w1_ref, w2_ref, w3_ref, xf, cotf):
    count = cot_ref.shape[0]
    shift_cot(cot_ref, cotf, [jnp.zeros((1, LANES), F32)] * 2)

    def block(i, _):
        r = pl.multiple_of(i * BLOCK, BLOCK)
        rows = pl.ds(r, BLOCK)
        some = pl.ds(pl.multiple_of(STRIDE * r, STRIDE * BLOCK), STRIDE * BLOCK)
        xf[some] = x_ref[some].astype(F32)
        for p in range(STRIDE):
            phase_ref[rows, p * LANES : (p + 1) * LANES] = xf[pl.ds(STRIDE * r + p, BLOCK, stride=STRIDE)].astype(BF)
        for k in range(2):
            next_ref[rows, k * LANES : (k + 1) * LANES] = cotf[k, pl.ds(r + 1, BLOCK)].astype(BF)
        return 0

    lax.fori_loop(0, count // BLOCK, block, 0)
    prepare(res_ref, proj_ref, down_ref, (w0_ref, w1_ref, w2_ref, w3_ref))


def edge(*rows):
    blank = jnp.zeros((EDGE - len(rows), rows[0].shape[1]), F32)
    return jnp.concatenate([*rows, blank], axis=0)


def first_kernel(
    scale, phase_ref, next_ref, cot_ref, behind_ref, w0_ref, w1_ref, w2_ref, w3_ref,
    mine_ref, other_ref, sq_ref, cots_ref, act3, act4, acc_res, acc_proj,
):
    count = cot_ref.shape[0]
    taps = STRIDE * LANES
    steps = count // BLOCK
    weights = (w0_ref, w1_ref, w2_ref, w3_ref)
    behind = behind_ref[...].astype(F32)
    acc_res[...] = jnp.zeros_like(acc_res)
    acc_proj[...] = jnp.zeros_like(acc_proj)
    for k, act in enumerate((act3, act4)):
        act[pl.ds(0, 8)] = jnp.broadcast_to(elu(behind[EDGE - 2 + k : EDGE - 1 + k, :LANES]), (8, LANES))

    def gather(at, result):
        inputs, squashed, grad_y, grad_h, hidden_act = result
        sq_ref[at] = lanes(*squashed)
        for k in range(3):
            n, m = inputs[k].shape[1], grad_y[k].shape[1]
            acc_res[:, :n] += dot_rows(grad_h[k], inputs[k])
            acc_proj[:, :m] += dot_rows(hidden_act[k], grad_y[k])

    cots_ref[pl.ds(0, count)] = lanes(next_ref[...], cot_ref[...])
    end = jnp.logical_and(lax.axis_index("z") == Z - 1, lax.axis_index("y") == Y - 1)
    mend = pl.ds(count - EDGE, EDGE)
    keep = jnp.logical_or(end, lax.broadcasted_iota(jnp.int32, (EDGE, 4 * LANES), 0) < EDGE - 1)
    cots_ref[mend] = jnp.where(keep, cots_ref[mend].astype(F32), 0.0).astype(BF)

    def block(i, _):
        r = pl.multiple_of(i * BLOCK, BLOCK)
        rows = pl.ds(r, BLOCK)
        xs = [phase_ref[rows, p * LANES : (p + 1) * LANES].astype(F32) for p in range(STRIDE)]
        acts = [elu(x) for x in xs]
        act3[pl.ds(r + 8, BLOCK)] = acts[3]
        act4[pl.ds(r + 8, BLOCK)] = acts[4]
        before = [a[pl.ds(r + 7, BLOCK)].astype(BF) for a in (act3, act4)]
        gather(rows, frames(xs, [a.astype(BF) for a in acts], before, cots_ref[rows], weights))
        return 0

    lax.fori_loop(0, steps, block, 0)
    xs = [edge(behind[11 + p : 12 + p, :LANES]) for p in range(STRIDE)]
    before = [edge(elu(behind[9 + k : 10 + k, :LANES])).astype(BF) for k in range(2)]
    first_cot = cot_ref[pl.ds(0, EDGE)].astype(F32)[0:1]
    cots = lanes(edge(first_cot), edge(behind[EDGE - 1 :, LANES:])).astype(BF)
    cots_ref[pl.ds(count, EDGE)] = cots
    gather(pl.ds(count, EDGE), frames(xs, [elu(x).astype(BF) for x in xs], before, cots, weights))

    half = LANES // 2
    core = lax.axis_index("core")

    def pack(part, at, value):
        size = value.shape[0]
        value = value.astype(BF)

        @pl.when(core == part)
        def _():
            mine_ref[pl.ds(at, size)] = value

        @pl.when(core != part)
        def _():
            other_ref[pl.ds(at, size)] = value

    for p in range(STRIDE):
        grads = dot_rows(sq_ref[:, p * LANES : (p + 1) * LANES], cots_ref[...]) * scale
        for k in range(4):
            pack(k // 2, (k % 2) * taps + p * LANES, grads[:, k * LANES : (k + 1) * LANES])
    small = [
        acc_res[:half, j * LANES : (j + 1) * LANES] + acc_res[half:, (j + 1) * LANES : (j + 2) * LANES] for j in range(3)
    ]
    small.append(acc_proj[:half, :LANES] + acc_proj[half:, LANES:])
    at = 2 * taps
    rest = jnp.zeros((mine_ref.shape[0] - at - 2 * half, LANES), F32)
    for k in range(2):
        pack(k, at, jnp.concatenate(small[2 * k : 2 * k + 2], axis=0) * scale)
        pack(k, at + 2 * half, rest)


def second_kernel(
    x_ref, cot_ref, behind_ref, ahead_ref, res_ref, proj_ref, down_ref,
    enc_ref, out_ref, xf, cotf, act3, act4, g0_ref, gh_ref, gy_ref, lead, mix_ref, w0_ref, w1_ref, w2_ref, w3_ref,
):
    length, count = x_ref.shape[0], cot_ref.shape[0]
    taps = STRIDE * LANES
    steps = count // BLOCK
    weights = (w0_ref, w1_ref, w2_ref, w3_ref)
    prepare(res_ref, proj_ref, down_ref, weights)
    w = [res_ref[j] for j in range(3)]
    zero = jnp.zeros_like(w[0])
    mix_ref[...] = jnp.concatenate(
        [
            lanes(w[2], zero, zero), lanes(w[1], w[2], zero), lanes(w[0], w[1], w[2]), lanes(zero, w[0], w[1]),
            lanes(zero, w[0], w[1]), lanes(zero, zero, w[0]),
        ],
        axis=0,
    )
    behind = behind_ref[...].astype(F32)
    ahead = ahead_ref[...].astype(F32)
    shift_cot(cot_ref, cotf, [ahead[0:1, (1 + k) * LANES : (2 + k) * LANES] for k in range(2)])
    for k, act in enumerate((act3, act4)):
        act[pl.ds(0, 8)] = jnp.broadcast_to(elu(behind[EDGE - 2 + k : EDGE - 1 + k, :LANES]), (8, LANES))
    w_lead, w_tail = down_ref.at[pl.ds(0, taps)], down_ref.at[pl.ds(taps, taps)]

    def encode(r, squashed):
        first = dot(squashed, w_lead[...])
        for k in range(2):
            lead[k, pl.ds(r + 8, BLOCK)] = first[:, k * LANES : (k + 1) * LANES]
        shifted = lanes(*[lead[k, pl.ds(r + 7, BLOCK)] for k in range(2)])
        enc_ref[pl.ds(r, BLOCK)] = (shifted + dot(squashed, w_tail[...])).astype(BF)

    xs = [edge(behind[11 + p : 12 + p, :LANES]) for p in range(STRIDE)]
    before = [edge(elu(behind[9 + k : 10 + k, :LANES])).astype(BF) for k in range(2)]
    cots = jnp.zeros((EDGE, 4 * LANES), BF)
    _, squashed, _, _, _ = frames(xs, [elu(x).astype(BF) for x in xs], before, cots, weights)
    start = dot(lanes(*squashed), w_lead[...])
    for k in range(2):
        lead[k, pl.ds(0, 8)] = jnp.broadcast_to(start[0:1, k * LANES : (k + 1) * LANES], (8, LANES))

    def forward(i, _):
        r = pl.multiple_of(i * BLOCK, BLOCK)
        rows = pl.ds(r, BLOCK)
        some = pl.ds(pl.multiple_of(STRIDE * r, STRIDE * BLOCK), STRIDE * BLOCK)
        xf[some] = x_ref[some].astype(F32)
        xs = [xf[pl.ds(STRIDE * r + p, BLOCK, stride=STRIDE)] for p in range(STRIDE)]
        acts = [elu(x) for x in xs]
        act3[pl.ds(r + 8, BLOCK)] = acts[3]
        act4[pl.ds(r + 8, BLOCK)] = acts[4]
        before = [a[pl.ds(r + 7, BLOCK)].astype(BF) for a in (act3, act4)]
        cot_next = [cotf[k, pl.ds(r + 1, BLOCK)].astype(BF) for k in range(2)]
        _, squashed, grad_y, grad_h, _ = frames(
            xs, [a.astype(BF) for a in acts], before, lanes(*cot_next, cot_ref[rows]), weights
        )
        encode(r, lanes(*squashed))
        gy_ref[rows] = lanes(*grad_y)
        gh_ref[rows] = lanes(*grad_h)
        g0_ref[rows] = grad_h[0].astype(F32)
        return 0

    lax.fori_loop(0, steps, forward, 0)
    blank = jnp.zeros((1, LANES), F32)
    xs = [edge(ahead[p : p + 1, :LANES] if p < 2 else blank) for p in range(STRIDE)]
    before = [edge(act[pl.ds(count, 8)][7:8]).astype(BF) for act in (act3, act4)]
    cots = lanes(edge(ahead[1:2, LANES:]), edge(ahead[0:1, LANES:])).astype(BF)
    _, _, _, grad_h, _ = frames(xs, [elu(x).astype(BF) for x in xs], before, cots, weights)
    g0_ref[pl.ds(count, 8)] = grad_h[0].astype(F32)[:8]

    def backward(i, _):
        r = pl.multiple_of(i * BLOCK, BLOCK)
        rows = pl.ds(r, BLOCK)
        grad_h = gh_ref[rows]
        later = g0_ref[pl.ds(r + 1, BLOCK)].astype(BF)
        grad_a = lanes(
            dot(grad_h[:, : 2 * LANES], mix_ref[: 2 * LANES, : 2 * LANES]),
            dot(lanes(grad_h[:, LANES:], later), mix_ref[...]),
        )
        for p in range(STRIDE):
            here = pl.ds(STRIDE * r + p, BLOCK, stride=STRIDE)
            own = slice(p * LANES, (p + 1) * LANES)
            xf[here] = gy_ref[rows, own].astype(F32) + grad_a[:, own] * slope_of(xf[here])
        some = pl.ds(pl.multiple_of(STRIDE * r, STRIDE * BLOCK), STRIDE * BLOCK)
        out_ref[some] = xf[some].astype(BF)
        return 0

    lax.fori_loop(0, steps, backward, 0)


def last_kernel(mine_ref, other_ref, res_ref, proj_ref, down_ref):
    taps, half = STRIDE * LANES, LANES // 2
    core = lax.axis_index("core")

    def unpack(ref, part):
        for k in range(2):
            for p in range(STRIDE):
                block = ref[pl.ds(k * taps + p * LANES, LANES)].astype(F32)
                down_ref[STRIDE * part + p, :, pl.ds(k * LANES, LANES)] = block
        small = [ref[pl.ds(2 * taps + k * half, half)].astype(F32) for k in range(2)]
        res_ref[2 * part] = small[0]
        if part == 0:
            res_ref[1] = small[1]
        else:
            proj_ref[...] = small[1]

    for first, second, held in ((mine_ref, other_ref, 0), (other_ref, mine_ref, 1)):

        @pl.when(core == held)
        def _():
            unpack(first, 0)
            unpack(second, 1)


def second_call(x, cot, behind, ahead, w_res, w_proj, down):
    (length, channels), (count, out_width) = x.shape, cot.shape
    taps = STRIDE * channels
    return pl.pallas_call(
        second_kernel,
        out_shape=(shape(count, out_width), shape(length, channels)),
        in_specs=[VMEM] * 7,
        out_specs=(VMEM,) * 2,
        scratch_shapes=[
            pltpu.VMEM((length, LANES), F32),
            pltpu.VMEM((2, count + 8, LANES), F32),
            pltpu.VMEM((count + 8, LANES), F32),
            pltpu.VMEM((count + 8, LANES), F32),
            pltpu.VMEM((count + 8, LANES), F32),
            pltpu.VMEM((count, 3 * LANES), BF),
            pltpu.VMEM((count, taps), BF),
            pltpu.VMEM((2, count + 8, LANES), F32),
            pltpu.VMEM((3 * LANES, 3 * LANES), BF),
            pltpu.VMEM((4 * LANES, LANES), BF),
            pltpu.VMEM((LANES, 2 * LANES), BF),
            pltpu.VMEM((2 * LANES, LANES), BF),
            pltpu.VMEM((4 * LANES, taps), BF),
        ],
        compiler_params=pltpu.CompilerParams(vmem_limit_bytes=LIMIT),
        cost_estimate=pl.CostEstimate(flops=3 * 10**9, bytes_accessed=10**7, transcendentals=3 * 10**6),
        name="second",
    )(x, cot, behind, ahead, w_res, w_proj, down)


def shards(samples, w_res, w_proj, w_down, cotangent):
    clip_count, length, channels = samples.shape
    frame_count, out_width = cotangent.shape[1:]
    hid_width = w_proj.shape[0]
    taps = STRIDE * channels
    x, cot = samples[0], cotangent[0]
    down = w_down.reshape(2 * taps, out_width)
    w_res = jnp.transpose(w_res, (0, 2, 1))
    tail, head = pl.pallas_call(
        rim_kernel,
        out_shape=(shape(EDGE, 3 * LANES), shape(EDGE, 3 * LANES)),
        in_specs=[ANY] * 2,
        out_specs=(VMEM,) * 2,
        scratch_shapes=[pltpu.SemaphoreType.DMA((4,))],
        compiler_params=pltpu.CompilerParams(vmem_limit_bytes=62_000_000),
        name="rim",
    )(x, cot)
    behind = from_behind(tail, 1)
    phases, cot_next, *weights = pl.pallas_call(
        pre_kernel,
        out_shape=(
            shape(frame_count, taps), shape(frame_count, out_width), shape(4 * LANES, LANES), shape(LANES, 2 * LANES),
            shape(2 * LANES, LANES), shape(4 * LANES, taps),
        ),
        in_specs=[VMEM] * 5,
        out_specs=(VMEM,) * 6,
        scratch_shapes=[pltpu.VMEM((length, LANES), F32), pltpu.VMEM((2, frame_count + 8, LANES), F32)],
        compiler_params=pltpu.CompilerParams(vmem_limit_bytes=LIMIT),
        cost_estimate=pl.CostEstimate(flops=10**7, bytes_accessed=6 * 10**6, transcendentals=655360),
        name="pre",
    )(x, cot, w_res, w_proj, down)
    size = 2 * taps * out_width + 3 * channels * hid_width + hid_width * channels
    parts = X * Y * EDGE
    rows = -(-size // (2 * LANES * parts)) * parts
    scale = 1.0 / math.sqrt(clip_count * XC * frame_count * Y * Z)
    mine, other = pl.pallas_call(
        functools.partial(first_kernel, scale),
        out_shape=(shape(rows, LANES), shape(rows, LANES)),
        in_specs=[VMEM] * 8,
        out_specs=(VMEM,) * 2,
        scratch_shapes=[
            pltpu.VMEM((frame_count + EDGE, taps), BF),
            pltpu.VMEM((frame_count + EDGE, 2 * out_width), BF),
            pltpu.VMEM((frame_count + 8, LANES), F32),
            pltpu.VMEM((frame_count + 8, LANES), F32),
            pltpu.VMEM((LANES, 4 * LANES), F32),
            pltpu.VMEM((LANES, 2 * LANES), F32),
        ],
        compiler_params=pltpu.CompilerParams(vmem_limit_bytes=LIMIT),
        cost_estimate=pl.CostEstimate(flops=3 * 10**9, bytes_accessed=8 * 10**6, transcendentals=2 * 10**6),
        name="first",
    )(phases, cot_next, cot, behind, *weights)
    other, ahead = lax.optimization_barrier((other, from_behind(head, -1)))
    mine, other, (encoded, d_input) = total(mine, other, (x, cot, behind, ahead, w_res, w_proj, down))
    grad_res, grad_proj, grad_down = pl.pallas_call(
        last_kernel,
        out_shape=(
            jax.ShapeDtypeStruct((3, hid_width, channels), F32),
            jax.ShapeDtypeStruct((hid_width, channels), F32),
            jax.ShapeDtypeStruct((2 * STRIDE, channels, out_width), F32),
        ),
        in_specs=[VMEM] * 2,
        out_specs=(VMEM,) * 3,
        compiler_params=pltpu.CompilerParams(vmem_limit_bytes=LIMIT),
        name="last",
    )(mine, other)
    return (encoded[None], d_input[None], jnp.transpose(grad_res, (0, 2, 1)), grad_proj, grad_down)


def solution(mesh):
    mesh = Mesh(mesh.devices.reshape(X, CORE, Z, Y), ("x", "core", "z", "y"))
    data = P(("x", "core"), TM, None)
    in_specs = (data, P(), P(), P(), data)
    out_specs = (data, data, P(), P(), P())
    return jax.shard_map(shards, mesh=mesh, in_specs=in_specs, out_specs=out_specs, check_vma=False)
```

```python
import functools
import math

import jax
import jax.numpy as jnp
from jax import lax
from jax.experimental import pallas as pl
from jax.experimental.pallas import tpu as pltpu
from jax.sharding import Mesh, PartitionSpec as P

STRIDE = 5
X, CORE, Z, Y = 4, 2, 8, 8
XC = X * CORE
LANES = 128
EDGE = 16
BLOCK = 1024
LIMIT = 32 * 2**20
TM = ("z", "y")
BF = jnp.bfloat16
F32 = jnp.float32
VMEM = pl.BlockSpec(memory_space=pltpu.VMEM)
ANY = pl.BlockSpec(memory_space=pltpu.HBM)


def shape(rows, columns, kind=BF):
    return jax.ShapeDtypeStruct((rows, columns), kind)


def from_behind(value, steps):
    count = Z * Y
    first, last = (max(0, -steps), min(count, count - steps))
    return lax.ppermute(value, TM, [(source, source + steps) for source in range(first, last)])


def exchange(blocks, axes):
    return lax.all_to_all(blocks, axes, 0, 0, tiled=True)


def copies(value, axes, count):
    return exchange(jnp.broadcast_to(value[None], (count,) + value.shape), axes)


def swap(value):
    return lax.ppermute(value, "core", [(0, 1), (1, 0)])


def total(mine, other, head, beside, weights):
    part = (mine.astype(F32) + swap(other).astype(F32)).astype(BF)
    part = jnp.sum(exchange(part.reshape(X * Y, -1, LANES), ("x", "y")).astype(F32), axis=0).astype(BF)
    part, head = lax.optimization_barrier((part, head))
    ahead = from_behind(head, -1)
    part = jnp.sum(copies(part, "z", Z).astype(F32), axis=0).astype(BF)
    part, ahead = lax.optimization_barrier((part, ahead))
    outputs = second_call(*beside, ahead, *weights)
    part = copies(part, ("x", "y"), X * Y).reshape(-1, LANES)
    part, *outputs = lax.optimization_barrier((part, *outputs))
    return part, swap(part), outputs


def dot(a, b):
    return jnp.dot(a, b, preferred_element_type=F32)


def dot_rows(a, b):
    return lax.dot_general(a, b, (((0,), (0,)), ((), ())), preferred_element_type=F32)


def slope_of(v):
    return jnp.exp(jnp.minimum(v, 0.0))


def elu_of(v, slope):
    return jnp.maximum(v, 0.0) + (slope - 1.0)


def elu(v):
    return elu_of(v, slope_of(v))


def lanes(*pieces):
    return jnp.concatenate(pieces, axis=1)


def rim_kernel(x_hbm, cot_hbm, tail_ref, head_ref, sem):
    size, end, last = EDGE, x_hbm.shape[0] - EDGE, cot_hbm.shape[0] - EDGE
    moves = (
        (x_hbm.at[pl.ds(end, size)], tail_ref.at[:, pl.ds(0, LANES)]),
        (cot_hbm.at[pl.ds(last, size)], tail_ref.at[:, pl.ds(LANES, 2 * LANES)]),
        (x_hbm.at[pl.ds(0, size)], head_ref.at[:, pl.ds(0, LANES)]),
        (cot_hbm.at[pl.ds(0, size)], head_ref.at[:, pl.ds(LANES, 2 * LANES)]),
    )
    moves = [pltpu.make_async_copy(source, target, sem.at[k]) for k, (source, target) in enumerate(moves)]
    for move in moves:
        move.start()
    for move in moves:
        move.wait()


def frames(xs, acts, before, cots, weights):
    w_conv, w_pair, w_back, w_grad = [w[...] for w in weights]
    inputs = (
        lanes(before[0], before[1], acts[0], acts[1]),
        lanes(acts[0], acts[1], acts[2], acts[3]),
        lanes(acts[2], acts[3], acts[4]),
    )
    grad_sq = dot(cots, w_grad)
    squashed, grad_y, grad_h, hidden_act = [], [], [], []
    for pair, stacked in enumerate(inputs):
        wide = 2 if pair < 2 else 1
        hidden = dot(stacked, w_conv[: stacked.shape[1]])
        if wide == 1:
            hidden = jnp.where(lax.broadcasted_iota(jnp.int32, hidden.shape, 1) < LANES // 2, hidden, 0.0)
        slope_h = slope_of(hidden)
        act_h = elu_of(hidden, slope_h).astype(BF)
        branch = dot(act_h, w_pair[:, : wide * LANES])
        own = []
        for k in range(wide):
            p = 2 * pair + k
            res = (xs[p] + branch[:, k * LANES : (k + 1) * LANES]).astype(BF).astype(F32)
            slope_r = slope_of(res)
            squashed.append(elu_of(res, slope_r).astype(BF))
            own.append((grad_sq[:, p * LANES : (p + 1) * LANES] * slope_r).astype(BF))
        own = own[0] if wide == 1 else lanes(*own)
        grad_y.append(own)
        grad_h.append((dot(own, w_back[: wide * LANES]) * slope_h).astype(BF))
        hidden_act.append(act_h)
    return inputs, squashed, grad_y, grad_h, hidden_act


def prepare(res_ref, proj_ref, down_ref, weights):
    w_conv, w_pair, w_back, w_grad = weights
    taps = STRIDE * LANES
    w = [res_ref[j] for j in range(3)]
    zero = jnp.zeros_like(w[0])
    above = (*w, zero)
    below = (zero, *w)
    for k in range(4):
        block = jnp.concatenate([above[k], below[k]], axis=0)
        w_conv[pl.ds(k * LANES, LANES)] = jnp.transpose(block)
    proj = proj_ref[...]
    none = jnp.zeros_like(proj)
    for k in range(2):
        block = jnp.concatenate([none, proj] if k else [proj, none], axis=0)
        w_pair[:, pl.ds(k * LANES, LANES)] = block
        w_back[pl.ds(k * LANES, LANES)] = jnp.transpose(block)
    for part in range(2):
        for p in range(STRIDE):
            for k in range(2):
                block = down_ref[pl.ds(part * taps + p * LANES, LANES), pl.ds(k * LANES, LANES)]
                w_grad[pl.ds((2 * part + k) * LANES, LANES), pl.ds(p * LANES, LANES)] = jnp.transpose(block)


def shift_cot(cot_ref, cotf, last):
    count = cot_ref.shape[0]
    for k in range(2):
        cotf[k, pl.ds(0, count)] = cot_ref[:, k * LANES : (k + 1) * LANES].astype(F32)
        cotf[k, pl.ds(count, 8)] = jnp.broadcast_to(last[k], (8, LANES))


def pre_kernel(x_ref, cot_ref, res_ref, proj_ref, down_ref, phase_ref, next_ref, w0_ref, w1_ref, w2_ref, w3_ref, xf, cotf):
    count = cot_ref.shape[0]
    shift_cot(cot_ref, cotf, [jnp.zeros((1, LANES), F32)] * 2)

    def block(i, _):
        r = pl.multiple_of(i * BLOCK, BLOCK)
        rows = pl.ds(r, BLOCK)
        some = pl.ds(pl.multiple_of(STRIDE * r, STRIDE * BLOCK), STRIDE * BLOCK)
        xf[some] = x_ref[some].astype(F32)
        for p in range(STRIDE):
            phase_ref[rows, p * LANES : (p + 1) * LANES] = xf[pl.ds(STRIDE * r + p, BLOCK, stride=STRIDE)].astype(BF)
        for k in range(2):
            next_ref[rows, k * LANES : (k + 1) * LANES] = cotf[k, pl.ds(r + 1, BLOCK)].astype(BF)
        return 0

    lax.fori_loop(0, count // BLOCK, block, 0)
    prepare(res_ref, proj_ref, down_ref, (w0_ref, w1_ref, w2_ref, w3_ref))


def edge(*rows):
    blank = jnp.zeros((EDGE - len(rows), rows[0].shape[1]), F32)
    return jnp.concatenate([*rows, blank], axis=0)


def first_kernel(
    scale, phase_ref, next_ref, cot_ref, behind_ref, w0_ref, w1_ref, w2_ref, w3_ref,
    mine_ref, other_ref, sq_ref, cots_ref, act3, act4, acc_res, acc_proj,
):
    count = cot_ref.shape[0]
    taps = STRIDE * LANES
    steps = count // BLOCK
    weights = (w0_ref, w1_ref, w2_ref, w3_ref)
    behind = behind_ref[...].astype(F32)
    acc_res[...] = jnp.zeros_like(acc_res)
    acc_proj[...] = jnp.zeros_like(acc_proj)
    for k, act in enumerate((act3, act4)):
        act[pl.ds(0, 8)] = jnp.broadcast_to(elu(behind[EDGE - 2 + k : EDGE - 1 + k, :LANES]), (8, LANES))

    def gather(at, result):
        inputs, squashed, grad_y, grad_h, hidden_act = result
        sq_ref[at] = lanes(*squashed)
        for k in range(3):
            n, m = inputs[k].shape[1], grad_y[k].shape[1]
            acc_res[:, :n] += dot_rows(grad_h[k], inputs[k])
            acc_proj[:, :m] += dot_rows(hidden_act[k], grad_y[k])

    cots_ref[pl.ds(0, count)] = lanes(next_ref[...], cot_ref[...])
    end = jnp.logical_and(lax.axis_index("z") == Z - 1, lax.axis_index("y") == Y - 1)
    mend = pl.ds(count - EDGE, EDGE)
    keep = jnp.logical_or(end, lax.broadcasted_iota(jnp.int32, (EDGE, 4 * LANES), 0) < EDGE - 1)
    cots_ref[mend] = jnp.where(keep, cots_ref[mend].astype(F32), 0.0).astype(BF)

    def block(i, _):
        r = pl.multiple_of(i * BLOCK, BLOCK)
        rows = pl.ds(r, BLOCK)
        xs = [phase_ref[rows, p * LANES : (p + 1) * LANES].astype(F32) for p in range(STRIDE)]
        acts = [elu(x) for x in xs]
        act3[pl.ds(r + 8, BLOCK)] = acts[3]
        act4[pl.ds(r + 8, BLOCK)] = acts[4]
        before = [a[pl.ds(r + 7, BLOCK)].astype(BF) for a in (act3, act4)]
        gather(rows, frames(xs, [a.astype(BF) for a in acts], before, cots_ref[rows], weights))
        return 0

    lax.fori_loop(0, steps, block, 0)
    xs = [edge(behind[11 + p : 12 + p, :LANES]) for p in range(STRIDE)]
    before = [edge(elu(behind[9 + k : 10 + k, :LANES])).astype(BF) for k in range(2)]
    first_cot = cot_ref[pl.ds(0, EDGE)].astype(F32)[0:1]
    cots = lanes(edge(first_cot), edge(behind[EDGE - 1 :, LANES:])).astype(BF)
    cots_ref[pl.ds(count, EDGE)] = cots
    gather(pl.ds(count, EDGE), frames(xs, [elu(x).astype(BF) for x in xs], before, cots, weights))

    half = LANES // 2
    core = lax.axis_index("core")

    def pack(part, at, value):
        size = value.shape[0]
        value = value.astype(BF)

        @pl.when(core == part)
        def _():
            mine_ref[pl.ds(at, size)] = value

        @pl.when(core != part)
        def _():
            other_ref[pl.ds(at, size)] = value

    for p in range(STRIDE):
        grads = dot_rows(sq_ref[:, p * LANES : (p + 1) * LANES], cots_ref[...]) * scale
        for k in range(4):
            pack(k // 2, (k % 2) * taps + p * LANES, grads[:, k * LANES : (k + 1) * LANES])
    small = [
        acc_res[:half, j * LANES : (j + 1) * LANES] + acc_res[half:, (j + 1) * LANES : (j + 2) * LANES] for j in range(3)
    ]
    small.append(acc_proj[:half, :LANES] + acc_proj[half:, LANES:])
    at = 2 * taps
    rest = jnp.zeros((mine_ref.shape[0] - at - 2 * half, LANES), F32)
    for k in range(2):
        pack(k, at, jnp.concatenate(small[2 * k : 2 * k + 2], axis=0) * scale)
        pack(k, at + 2 * half, rest)


def second_kernel(
    x_ref, cot_ref, behind_ref, ahead_ref, res_ref, proj_ref, down_ref,
    enc_ref, out_ref, xf, cotf, act3, act4, g0_ref, gh_ref, gy_ref, lead, mix_ref, w0_ref, w1_ref, w2_ref, w3_ref,
):
    length, count = x_ref.shape[0], cot_ref.shape[0]
    taps = STRIDE * LANES
    steps = count // BLOCK
    weights = (w0_ref, w1_ref, w2_ref, w3_ref)
    prepare(res_ref, proj_ref, down_ref, weights)
    w = [res_ref[j] for j in range(3)]
    zero = jnp.zeros_like(w[0])
    mix_ref[...] = jnp.concatenate(
        [
            lanes(w[2], zero, zero), lanes(w[1], w[2], zero), lanes(w[0], w[1], w[2]), lanes(zero, w[0], w[1]),
            lanes(zero, w[0], w[1]), lanes(zero, zero, w[0]),
        ],
        axis=0,
    )
    behind = behind_ref[...].astype(F32)
    ahead = ahead_ref[...].astype(F32)
    shift_cot(cot_ref, cotf, [ahead[0:1, (1 + k) * LANES : (2 + k) * LANES] for k in range(2)])
    for k, act in enumerate((act3, act4)):
        act[pl.ds(0, 8)] = jnp.broadcast_to(elu(behind[EDGE - 2 + k : EDGE - 1 + k, :LANES]), (8, LANES))
    w_lead, w_tail = down_ref.at[pl.ds(0, taps)], down_ref.at[pl.ds(taps, taps)]

    def encode(r, squashed):
        first = dot(squashed, w_lead[...])
        for k in range(2):
            lead[k, pl.ds(r + 8, BLOCK)] = first[:, k * LANES : (k + 1) * LANES]
        shifted = lanes(*[lead[k, pl.ds(r + 7, BLOCK)] for k in range(2)])
        enc_ref[pl.ds(r, BLOCK)] = (shifted + dot(squashed, w_tail[...])).astype(BF)

    xs = [edge(behind[11 + p : 12 + p, :LANES]) for p in range(STRIDE)]
    before = [edge(elu(behind[9 + k : 10 + k, :LANES])).astype(BF) for k in range(2)]
    cots = jnp.zeros((EDGE, 4 * LANES), BF)
    _, squashed, _, _, _ = frames(xs, [elu(x).astype(BF) for x in xs], before, cots, weights)
    start = dot(lanes(*squashed), w_lead[...])
    for k in range(2):
        lead[k, pl.ds(0, 8)] = jnp.broadcast_to(start[0:1, k * LANES : (k + 1) * LANES], (8, LANES))

    def forward(i, _):
        r = pl.multiple_of(i * BLOCK, BLOCK)
        rows = pl.ds(r, BLOCK)
        some = pl.ds(pl.multiple_of(STRIDE * r, STRIDE * BLOCK), STRIDE * BLOCK)
        xf[some] = x_ref[some].astype(F32)
        xs = [xf[pl.ds(STRIDE * r + p, BLOCK, stride=STRIDE)] for p in range(STRIDE)]
        acts = [elu(x) for x in xs]
        act3[pl.ds(r + 8, BLOCK)] = acts[3]
        act4[pl.ds(r + 8, BLOCK)] = acts[4]
        before = [a[pl.ds(r + 7, BLOCK)].astype(BF) for a in (act3, act4)]
        cot_next = [cotf[k, pl.ds(r + 1, BLOCK)].astype(BF) for k in range(2)]
        _, squashed, grad_y, grad_h, _ = frames(
            xs, [a.astype(BF) for a in acts], before, lanes(*cot_next, cot_ref[rows]), weights
        )
        encode(r, lanes(*squashed))
        gy_ref[rows] = lanes(*grad_y)
        gh_ref[rows] = lanes(*grad_h)
        g0_ref[rows] = grad_h[0].astype(F32)
        return 0

    lax.fori_loop(0, steps, forward, 0)
    blank = jnp.zeros((1, LANES), F32)
    xs = [edge(ahead[p : p + 1, :LANES] if p < 2 else blank) for p in range(STRIDE)]
    before = [edge(act[pl.ds(count, 8)][7:8]).astype(BF) for act in (act3, act4)]
    cots = lanes(edge(ahead[1:2, LANES:]), edge(ahead[0:1, LANES:])).astype(BF)
    _, _, _, grad_h, _ = frames(xs, [elu(x).astype(BF) for x in xs], before, cots, weights)
    g0_ref[pl.ds(count, 8)] = grad_h[0].astype(F32)[:8]

    def backward(i, _):
        r = pl.multiple_of(i * BLOCK, BLOCK)
        rows = pl.ds(r, BLOCK)
        grad_h = gh_ref[rows]
        later = g0_ref[pl.ds(r + 1, BLOCK)].astype(BF)
        grad_a = lanes(
            dot(grad_h[:, : 2 * LANES], mix_ref[: 2 * LANES, : 2 * LANES]),
            dot(lanes(grad_h[:, LANES:], later), mix_ref[...]),
        )
        for p in range(STRIDE):
            here = pl.ds(STRIDE * r + p, BLOCK, stride=STRIDE)
            own = slice(p * LANES, (p + 1) * LANES)
            xf[here] = gy_ref[rows, own].astype(F32) + grad_a[:, own] * slope_of(xf[here])
        some = pl.ds(pl.multiple_of(STRIDE * r, STRIDE * BLOCK), STRIDE * BLOCK)
        out_ref[some] = xf[some].astype(BF)
        return 0

    lax.fori_loop(0, steps, backward, 0)


def last_kernel(mine_ref, other_ref, res_ref, proj_ref, down_ref):
    taps, half = STRIDE * LANES, LANES // 2
    core = lax.axis_index("core")

    def unpack(ref, part):
        for k in range(2):
            for p in range(STRIDE):
                block = ref[pl.ds(k * taps + p * LANES, LANES)].astype(F32)
                down_ref[STRIDE * part + p, :, pl.ds(k * LANES, LANES)] = block
        small = [ref[pl.ds(2 * taps + k * half, half)].astype(F32) for k in range(2)]
        res_ref[2 * part] = small[0]
        if part == 0:
            res_ref[1] = small[1]
        else:
            proj_ref[...] = small[1]

    for first, second, held in ((mine_ref, other_ref, 0), (other_ref, mine_ref, 1)):

        @pl.when(core == held)
        def _():
            unpack(first, 0)
            unpack(second, 1)


def second_call(x, cot, behind, ahead, w_res, w_proj, down):
    (length, channels), (count, out_width) = x.shape, cot.shape
    taps = STRIDE * channels
    return pl.pallas_call(
        second_kernel,
        out_shape=(shape(count, out_width), shape(length, channels)),
        in_specs=[VMEM] * 7,
        out_specs=(VMEM,) * 2,
        scratch_shapes=[
            pltpu.VMEM((length, LANES), F32),
            pltpu.VMEM((2, count + 8, LANES), F32),
            pltpu.VMEM((count + 8, LANES), F32),
            pltpu.VMEM((count + 8, LANES), F32),
            pltpu.VMEM((count + 8, LANES), F32),
            pltpu.VMEM((count, 3 * LANES), BF),
            pltpu.VMEM((count, taps), BF),
            pltpu.VMEM((2, count + 8, LANES), F32),
            pltpu.VMEM((3 * LANES, 3 * LANES), BF),
            pltpu.VMEM((4 * LANES, LANES), BF),
            pltpu.VMEM((LANES, 2 * LANES), BF),
            pltpu.VMEM((2 * LANES, LANES), BF),
            pltpu.VMEM((4 * LANES, taps), BF),
        ],
        compiler_params=pltpu.CompilerParams(vmem_limit_bytes=LIMIT),
        cost_estimate=pl.CostEstimate(flops=3 * 10**9, bytes_accessed=10**7, transcendentals=3 * 10**6),
        name="second",
    )(x, cot, behind, ahead, w_res, w_proj, down)


def shards(samples, w_res, w_proj, w_down, cotangent):
    clip_count, length, channels = samples.shape
    frame_count, out_width = cotangent.shape[1:]
    hid_width = w_proj.shape[0]
    taps = STRIDE * channels
    x, cot = samples[0], cotangent[0]
    down = w_down.reshape(2 * taps, out_width)
    w_res = jnp.transpose(w_res, (0, 2, 1))
    tail, head = pl.pallas_call(
        rim_kernel,
        out_shape=(shape(EDGE, 3 * LANES), shape(EDGE, 3 * LANES)),
        in_specs=[ANY] * 2,
        out_specs=(VMEM,) * 2,
        scratch_shapes=[pltpu.SemaphoreType.DMA((4,))],
        compiler_params=pltpu.CompilerParams(vmem_limit_bytes=62_000_000),
        name="rim",
    )(x, cot)
    behind = from_behind(tail, 1)
    phases, cot_next, *weights = pl.pallas_call(
        pre_kernel,
        out_shape=(
            shape(frame_count, taps), shape(frame_count, out_width), shape(4 * LANES, LANES), shape(LANES, 2 * LANES),
            shape(2 * LANES, LANES), shape(4 * LANES, taps),
        ),
        in_specs=[VMEM] * 5,
        out_specs=(VMEM,) * 6,
        scratch_shapes=[pltpu.VMEM((length, LANES), F32), pltpu.VMEM((2, frame_count + 8, LANES), F32)],
        compiler_params=pltpu.CompilerParams(vmem_limit_bytes=LIMIT),
        cost_estimate=pl.CostEstimate(flops=10**7, bytes_accessed=6 * 10**6, transcendentals=655360),
        name="pre",
    )(x, cot, w_res, w_proj, down)
    size = 2 * taps * out_width + 3 * channels * hid_width + hid_width * channels
    parts = X * Y * EDGE
    rows = -(-size // (2 * LANES * parts)) * parts
    scale = 1.0 / math.sqrt(clip_count * XC * frame_count * Y * Z)
    mine, other = pl.pallas_call(
        functools.partial(first_kernel, scale),
        out_shape=(shape(rows, LANES), shape(rows, LANES)),
        in_specs=[VMEM] * 8,
        out_specs=(VMEM,) * 2,
        scratch_shapes=[
            pltpu.VMEM((frame_count + EDGE, taps), BF),
            pltpu.VMEM((frame_count + EDGE, 2 * out_width), BF),
            pltpu.VMEM((frame_count + 8, LANES), F32),
            pltpu.VMEM((frame_count + 8, LANES), F32),
            pltpu.VMEM((LANES, 4 * LANES), F32),
            pltpu.VMEM((LANES, 2 * LANES), F32),
        ],
        compiler_params=pltpu.CompilerParams(vmem_limit_bytes=LIMIT),
        cost_estimate=pl.CostEstimate(flops=3 * 10**9, bytes_accessed=8 * 10**6, transcendentals=2 * 10**6),
        name="first",
    )(phases, cot_next, cot, behind, *weights)
    mine, other, (encoded, d_input) = total(mine, other, head, (x, cot, behind), (w_res, w_proj, down))
    grad_res, grad_proj, grad_down = pl.pallas_call(
        last_kernel,
        out_shape=(
            jax.ShapeDtypeStruct((3, hid_width, channels), F32),
            jax.ShapeDtypeStruct((hid_width, channels), F32),
            jax.ShapeDtypeStruct((2 * STRIDE, channels, out_width), F32),
        ),
        in_specs=[VMEM] * 2,
        out_specs=(VMEM,) * 3,
        compiler_params=pltpu.CompilerParams(vmem_limit_bytes=LIMIT),
        name="last",
    )(mine, other)
    return (encoded[None], d_input[None], jnp.transpose(grad_res, (0, 2, 1)), grad_proj, grad_down)


def solution(mesh):
    mesh = Mesh(mesh.devices.reshape(X, CORE, Z, Y), ("x", "core", "z", "y"))
    data = P(("x", "core"), TM, None)
    in_specs = (data, P(), P(), P(), data)
    out_specs = (data, data, P(), P(), P())
    return jax.shard_map(shards, mesh=mesh, in_specs=in_specs, out_specs=out_specs, check_vma=False)
```

```python
import functools
import math

import jax
import jax.numpy as jnp
from jax import lax
from jax.experimental import pallas as pl
from jax.experimental.pallas import tpu as pltpu
from jax.sharding import Mesh, PartitionSpec as P

STRIDE = 5
X, CORE, Z, Y = 4, 2, 8, 8
XC = X * CORE
LANES = 128
EDGE = 16
BLOCK = 1024
LIMIT = 32 * 2**20
TM = ("z", "y")
BF = jnp.bfloat16
F32 = jnp.float32
VMEM = pl.BlockSpec(memory_space=pltpu.VMEM)
ANY = pl.BlockSpec(memory_space=pltpu.HBM)


def shape(rows, columns, kind=BF):
    return jax.ShapeDtypeStruct((rows, columns), kind)


def from_behind(value, steps):
    count = Z * Y
    first, last = (max(0, -steps), min(count, count - steps))
    return lax.ppermute(value, TM, [(source, source + steps) for source in range(first, last)])


def exchange(blocks, axes):
    return lax.all_to_all(blocks, axes, 0, 0, tiled=True)


def copies(value, axes, count):
    return exchange(jnp.broadcast_to(value[None], (count,) + value.shape), axes)


def swap(value):
    return lax.ppermute(value, "core", [(0, 1), (1, 0)])


def total(mine, other, head, beside, weights):
    part = (mine.astype(F32) + swap(other).astype(F32)).astype(BF)
    part = jnp.sum(exchange(part.reshape(X * Y, -1, LANES), ("x", "y")).astype(F32), axis=0).astype(BF)
    part, head = lax.optimization_barrier((part, head))
    ahead = from_behind(head, -1)
    part = jnp.sum(copies(part, "z", Z).astype(F32), axis=0).astype(BF)
    part, ahead = lax.optimization_barrier((part, ahead))
    outputs = second_call(*beside, ahead, *weights)
    part = copies(part, ("x", "y"), X * Y).reshape(-1, LANES)
    part, *outputs = lax.optimization_barrier((part, *outputs))
    return part, swap(part), outputs


def dot(a, b):
    return jnp.dot(a, b, preferred_element_type=F32)


def dot_rows(a, b):
    return lax.dot_general(a, b, (((0,), (0,)), ((), ())), preferred_element_type=F32)


def slope_of(v):
    return jnp.exp(jnp.minimum(v, 0.0))


def elu_of(v, slope):
    return jnp.maximum(v, 0.0) + (slope - 1.0)


def elu(v):
    return elu_of(v, slope_of(v))


def lanes(*pieces):
    return jnp.concatenate(pieces, axis=1)


def rim_kernel(x_hbm, cot_hbm, tail_ref, head_ref, sem):
    size, end, last = EDGE, x_hbm.shape[0] - EDGE, cot_hbm.shape[0] - EDGE
    moves = (
        (x_hbm.at[pl.ds(end, size)], tail_ref.at[:, pl.ds(0, LANES)]),
        (cot_hbm.at[pl.ds(last, size)], tail_ref.at[:, pl.ds(LANES, 2 * LANES)]),
        (x_hbm.at[pl.ds(0, size)], head_ref.at[:, pl.ds(0, LANES)]),
        (cot_hbm.at[pl.ds(0, size)], head_ref.at[:, pl.ds(LANES, 2 * LANES)]),
    )
    moves = [pltpu.make_async_copy(source, target, sem.at[k]) for k, (source, target) in enumerate(moves)]
    for move in moves:
        move.start()
    for move in moves:
        move.wait()


def frames(xs, acts, before, cots, weights):
    w_conv, w_pair, w_back, w_grad = [w[...] for w in weights]
    inputs = (
        lanes(before[0], before[1], acts[0], acts[1]),
        lanes(acts[0], acts[1], acts[2], acts[3]),
        lanes(acts[2], acts[3], acts[4]),
    )
    grad_sq = dot(cots, w_grad)
    squashed, grad_y, grad_h, hidden_act = [], [], [], []
    for pair, stacked in enumerate(inputs):
        wide = 2 if pair < 2 else 1
        hidden = dot(stacked, w_conv[: stacked.shape[1]])
        if wide == 1:
            hidden = jnp.where(lax.broadcasted_iota(jnp.int32, hidden.shape, 1) < LANES // 2, hidden, 0.0)
        slope_h = slope_of(hidden)
        act_h = elu_of(hidden, slope_h).astype(BF)
        branch = dot(act_h, w_pair[:, : wide * LANES])
        own = []
        for k in range(wide):
            p = 2 * pair + k
            res = (xs[p] + branch[:, k * LANES : (k + 1) * LANES]).astype(BF).astype(F32)
            slope_r = slope_of(res)
            squashed.append(elu_of(res, slope_r).astype(BF))
            own.append((grad_sq[:, p * LANES : (p + 1) * LANES] * slope_r).astype(BF))
        own = own[0] if wide == 1 else lanes(*own)
        grad_y.append(own)
        grad_h.append((dot(own, w_back[: wide * LANES]) * slope_h).astype(BF))
        hidden_act.append(act_h)
    return inputs, squashed, grad_y, grad_h, hidden_act


def prepare(res_ref, proj_ref, down_ref, weights):
    w_conv, w_pair, w_back, w_grad = weights
    taps = STRIDE * LANES
    w = [res_ref[j] for j in range(3)]
    zero = jnp.zeros_like(w[0])
    above = (*w, zero)
    below = (zero, *w)
    for k in range(4):
        block = jnp.concatenate([above[k], below[k]], axis=0)
        w_conv[pl.ds(k * LANES, LANES)] = jnp.transpose(block)
    proj = proj_ref[...]
    none = jnp.zeros_like(proj)
    for k in range(2):
        block = jnp.concatenate([none, proj] if k else [proj, none], axis=0)
        w_pair[:, pl.ds(k * LANES, LANES)] = block
        w_back[pl.ds(k * LANES, LANES)] = jnp.transpose(block)
    for part in range(2):
        for p in range(STRIDE):
            for k in range(2):
                block = down_ref[pl.ds(part * taps + p * LANES, LANES), pl.ds(k * LANES, LANES)]
                w_grad[pl.ds((2 * part + k) * LANES, LANES), pl.ds(p * LANES, LANES)] = jnp.transpose(block)


def shift_cot(cot_ref, cotf, last):
    count = cot_ref.shape[0]
    for k in range(2):
        cotf[k, pl.ds(0, count)] = cot_ref[:, k * LANES : (k + 1) * LANES].astype(F32)
        cotf[k, pl.ds(count, 8)] = jnp.broadcast_to(last[k], (8, LANES))


def pre_kernel(x_ref, cot_ref, res_ref, proj_ref, down_ref, phase_ref, next_ref, w0_ref, w1_ref, w2_ref, w3_ref, xf, cotf):
    count = cot_ref.shape[0]
    shift_cot(cot_ref, cotf, [jnp.zeros((1, LANES), F32)] * 2)

    def block(i, _):
        r = pl.multiple_of(i * BLOCK, BLOCK)
        rows = pl.ds(r, BLOCK)
        some = pl.ds(pl.multiple_of(STRIDE * r, STRIDE * BLOCK), STRIDE * BLOCK)
        xf[some] = x_ref[some].astype(F32)
        for p in range(STRIDE):
            phase_ref[rows, p * LANES : (p + 1) * LANES] = xf[pl.ds(STRIDE * r + p, BLOCK, stride=STRIDE)].astype(BF)
        for k in range(2):
            next_ref[rows, k * LANES : (k + 1) * LANES] = cotf[k, pl.ds(r + 1, BLOCK)].astype(BF)
        return 0

    lax.fori_loop(0, count // BLOCK, block, 0)
    prepare(res_ref, proj_ref, down_ref, (w0_ref, w1_ref, w2_ref, w3_ref))


def edge(*rows):
    blank = jnp.zeros((EDGE - len(rows), rows[0].shape[1]), F32)
    return jnp.concatenate([*rows, blank], axis=0)


def first_kernel(
    scale, phase_ref, next_ref, cot_ref, behind_ref, w0_ref, w1_ref, w2_ref, w3_ref,
    mine_ref, other_ref, sq_ref, cots_ref, act3, act4, acc_res, acc_proj,
):
    count = cot_ref.shape[0]
    taps = STRIDE * LANES
    weights = (w0_ref, w1_ref, w2_ref, w3_ref)
    behind = behind_ref[...].astype(F32)
    acc_res[...] = jnp.zeros_like(acc_res)
    acc_proj[...] = jnp.zeros_like(acc_proj)
    for k, act in enumerate((act3, act4)):
        act[pl.ds(0, 8)] = jnp.broadcast_to(elu(behind[EDGE - 2 + k : EDGE - 1 + k, :LANES]), (8, LANES))

    def gather(at, result):
        inputs, squashed, grad_y, grad_h, hidden_act = result
        sq_ref[at] = lanes(*squashed)
        for k in range(3):
            n, m = inputs[k].shape[1], grad_y[k].shape[1]
            acc_res[:, :n] += dot_rows(grad_h[k], inputs[k])
            acc_proj[:, :m] += dot_rows(hidden_act[k], grad_y[k])

    cots_ref[pl.ds(0, count)] = lanes(next_ref[...], cot_ref[...])
    end = jnp.logical_and(lax.axis_index("z") == Z - 1, lax.axis_index("y") == Y - 1)
    mend = pl.ds(count - EDGE, EDGE)
    keep = jnp.logical_or(end, lax.broadcasted_iota(jnp.int32, (EDGE, 4 * LANES), 0) < EDGE - 1)
    cots_ref[mend] = jnp.where(keep, cots_ref[mend].astype(F32), 0.0).astype(BF)
    first_cot = cot_ref[pl.ds(0, EDGE)].astype(F32)[0:1]
    cots_ref[pl.ds(count, EDGE)] = lanes(edge(first_cot), edge(behind[EDGE - 1 :, LANES:])).astype(BF)

    def join(main, rim):
        return jnp.concatenate([main, rim], axis=0)

    xs = [
        join(phase_ref[:, p * LANES : (p + 1) * LANES].astype(F32), edge(behind[11 + p : 12 + p, :LANES]))
        for p in range(STRIDE)
    ]
    acts = [elu(x) for x in xs]
    act3[pl.ds(8, count)] = acts[3][:count]
    act4[pl.ds(8, count)] = acts[4][:count]
    before = [
        join(act[pl.ds(7, count)], edge(elu(behind[9 + k : 10 + k, :LANES]))).astype(BF)
        for k, act in enumerate((act3, act4))
    ]
    every = pl.ds(0, count + EDGE)
    gather(every, frames(xs, [a.astype(BF) for a in acts], before, cots_ref[...], weights))

    half = LANES // 2
    core = lax.axis_index("core")

    def pack(part, at, value):
        size = value.shape[0]
        value = value.astype(BF)

        @pl.when(core == part)
        def _():
            mine_ref[pl.ds(at, size)] = value

        @pl.when(core != part)
        def _():
            other_ref[pl.ds(at, size)] = value

    for p in range(STRIDE):
        grads = dot_rows(sq_ref[:, p * LANES : (p + 1) * LANES], cots_ref[...]) * scale
        for k in range(4):
            pack(k // 2, (k % 2) * taps + p * LANES, grads[:, k * LANES : (k + 1) * LANES])
    small = [
        acc_res[:half, j * LANES : (j + 1) * LANES] + acc_res[half:, (j + 1) * LANES : (j + 2) * LANES] for j in range(3)
    ]
    small.append(acc_proj[:half, :LANES] + acc_proj[half:, LANES:])
    at = 2 * taps
    rest = jnp.zeros((mine_ref.shape[0] - at - 2 * half, LANES), F32)
    for k in range(2):
        pack(k, at, jnp.concatenate(small[2 * k : 2 * k + 2], axis=0) * scale)
        pack(k, at + 2 * half, rest)


def second_kernel(
    x_ref, cot_ref, behind_ref, ahead_ref, res_ref, proj_ref, down_ref,
    enc_ref, out_ref, xf, cotf, act3, act4, g0_ref, gh_ref, gy_ref, lead, mix_ref, w0_ref, w1_ref, w2_ref, w3_ref,
):
    length, count = x_ref.shape[0], cot_ref.shape[0]
    taps = STRIDE * LANES
    steps = count // BLOCK
    weights = (w0_ref, w1_ref, w2_ref, w3_ref)
    prepare(res_ref, proj_ref, down_ref, weights)
    w = [res_ref[j] for j in range(3)]
    zero = jnp.zeros_like(w[0])
    mix_ref[...] = jnp.concatenate(
        [
            lanes(w[2], zero, zero), lanes(w[1], w[2], zero), lanes(w[0], w[1], w[2]), lanes(zero, w[0], w[1]),
            lanes(zero, w[0], w[1]), lanes(zero, zero, w[0]),
        ],
        axis=0,
    )
    behind = behind_ref[...].astype(F32)
    ahead = ahead_ref[...].astype(F32)
    shift_cot(cot_ref, cotf, [ahead[0:1, (1 + k) * LANES : (2 + k) * LANES] for k in range(2)])
    for k, act in enumerate((act3, act4)):
        act[pl.ds(0, 8)] = jnp.broadcast_to(elu(behind[EDGE - 2 + k : EDGE - 1 + k, :LANES]), (8, LANES))
    w_lead, w_tail = down_ref.at[pl.ds(0, taps)], down_ref.at[pl.ds(taps, taps)]

    def encode(r, squashed):
        first = dot(squashed, w_lead[...])
        for k in range(2):
            lead[k, pl.ds(r + 8, BLOCK)] = first[:, k * LANES : (k + 1) * LANES]
        shifted = lanes(*[lead[k, pl.ds(r + 7, BLOCK)] for k in range(2)])
        enc_ref[pl.ds(r, BLOCK)] = (shifted + dot(squashed, w_tail[...])).astype(BF)

    xs = [edge(behind[11 + p : 12 + p, :LANES]) for p in range(STRIDE)]
    before = [edge(elu(behind[9 + k : 10 + k, :LANES])).astype(BF) for k in range(2)]
    cots = jnp.zeros((EDGE, 4 * LANES), BF)
    _, squashed, _, _, _ = frames(xs, [elu(x).astype(BF) for x in xs], before, cots, weights)
    start = dot(lanes(*squashed), w_lead[...])
    for k in range(2):
        lead[k, pl.ds(0, 8)] = jnp.broadcast_to(start[0:1, k * LANES : (k + 1) * LANES], (8, LANES))

    def forward(i, _):
        r = pl.multiple_of(i * BLOCK, BLOCK)
        rows = pl.ds(r, BLOCK)
        some = pl.ds(pl.multiple_of(STRIDE * r, STRIDE * BLOCK), STRIDE * BLOCK)
        xf[some] = x_ref[some].astype(F32)
        xs = [xf[pl.ds(STRIDE * r + p, BLOCK, stride=STRIDE)] for p in range(STRIDE)]
        acts = [elu(x) for x in xs]
        act3[pl.ds(r + 8, BLOCK)] = acts[3]
        act4[pl.ds(r + 8, BLOCK)] = acts[4]
        before = [a[pl.ds(r + 7, BLOCK)].astype(BF) for a in (act3, act4)]
        cot_next = [cotf[k, pl.ds(r + 1, BLOCK)].astype(BF) for k in range(2)]
        _, squashed, grad_y, grad_h, _ = frames(
            xs, [a.astype(BF) for a in acts], before, lanes(*cot_next, cot_ref[rows]), weights
        )
        encode(r, lanes(*squashed))
        gy_ref[rows] = lanes(*grad_y)
        gh_ref[rows] = lanes(*grad_h)
        g0_ref[rows] = grad_h[0].astype(F32)
        return 0

    lax.fori_loop(0, steps, forward, 0)
    blank = jnp.zeros((1, LANES), F32)
    xs = [edge(ahead[p : p + 1, :LANES] if p < 2 else blank) for p in range(STRIDE)]
    before = [edge(act[pl.ds(count, 8)][7:8]).astype(BF) for act in (act3, act4)]
    cots = lanes(edge(ahead[1:2, LANES:]), edge(ahead[0:1, LANES:])).astype(BF)
    _, _, _, grad_h, _ = frames(xs, [elu(x).astype(BF) for x in xs], before, cots, weights)
    g0_ref[pl.ds(count, 8)] = grad_h[0].astype(F32)[:8]

    def backward(i, _):
        r = pl.multiple_of(i * BLOCK, BLOCK)
        rows = pl.ds(r, BLOCK)
        grad_h = gh_ref[rows]
        later = g0_ref[pl.ds(r + 1, BLOCK)].astype(BF)
        grad_a = lanes(
            dot(grad_h[:, : 2 * LANES], mix_ref[: 2 * LANES, : 2 * LANES]),
            dot(lanes(grad_h[:, LANES:], later), mix_ref[...]),
        )
        for p in range(STRIDE):
            here = pl.ds(STRIDE * r + p, BLOCK, stride=STRIDE)
            own = slice(p * LANES, (p + 1) * LANES)
            xf[here] = gy_ref[rows, own].astype(F32) + grad_a[:, own] * slope_of(xf[here])
        some = pl.ds(pl.multiple_of(STRIDE * r, STRIDE * BLOCK), STRIDE * BLOCK)
        out_ref[some] = xf[some].astype(BF)
        return 0

    lax.fori_loop(0, steps, backward, 0)


def last_kernel(mine_ref, other_ref, res_ref, proj_ref, down_ref):
    taps, half = STRIDE * LANES, LANES // 2
    core = lax.axis_index("core")

    def unpack(ref, part):
        for k in range(2):
            for p in range(STRIDE):
                block = ref[pl.ds(k * taps + p * LANES, LANES)].astype(F32)
                down_ref[STRIDE * part + p, :, pl.ds(k * LANES, LANES)] = block
        small = [ref[pl.ds(2 * taps + k * half, half)].astype(F32) for k in range(2)]
        res_ref[2 * part] = small[0]
        if part == 0:
            res_ref[1] = small[1]
        else:
            proj_ref[...] = small[1]

    for first, second, held in ((mine_ref, other_ref, 0), (other_ref, mine_ref, 1)):

        @pl.when(core == held)
        def _():
            unpack(first, 0)
            unpack(second, 1)


def second_call(x, cot, behind, ahead, w_res, w_proj, down):
    (length, channels), (count, out_width) = x.shape, cot.shape
    taps = STRIDE * channels
    return pl.pallas_call(
        second_kernel,
        out_shape=(shape(count, out_width), shape(length, channels)),
        in_specs=[VMEM] * 7,
        out_specs=(VMEM,) * 2,
        scratch_shapes=[
            pltpu.VMEM((length, LANES), F32),
            pltpu.VMEM((2, count + 8, LANES), F32),
            pltpu.VMEM((count + 8, LANES), F32),
            pltpu.VMEM((count + 8, LANES), F32),
            pltpu.VMEM((count + 8, LANES), F32),
            pltpu.VMEM((count, 3 * LANES), BF),
            pltpu.VMEM((count, taps), BF),
            pltpu.VMEM((2, count + 8, LANES), F32),
            pltpu.VMEM((3 * LANES, 3 * LANES), BF),
            pltpu.VMEM((4 * LANES, LANES), BF),
            pltpu.VMEM((LANES, 2 * LANES), BF),
            pltpu.VMEM((2 * LANES, LANES), BF),
            pltpu.VMEM((4 * LANES, taps), BF),
        ],
        compiler_params=pltpu.CompilerParams(vmem_limit_bytes=LIMIT),
        cost_estimate=pl.CostEstimate(flops=3 * 10**9, bytes_accessed=10**7, transcendentals=3 * 10**6),
        name="second",
    )(x, cot, behind, ahead, w_res, w_proj, down)


def shards(samples, w_res, w_proj, w_down, cotangent):
    clip_count, length, channels = samples.shape
    frame_count, out_width = cotangent.shape[1:]
    hid_width = w_proj.shape[0]
    taps = STRIDE * channels
    x, cot = samples[0], cotangent[0]
    down = w_down.reshape(2 * taps, out_width)
    w_res = jnp.transpose(w_res, (0, 2, 1))
    tail, head = pl.pallas_call(
        rim_kernel,
        out_shape=(shape(EDGE, 3 * LANES), shape(EDGE, 3 * LANES)),
        in_specs=[ANY] * 2,
        out_specs=(VMEM,) * 2,
        scratch_shapes=[pltpu.SemaphoreType.DMA((4,))],
        compiler_params=pltpu.CompilerParams(vmem_limit_bytes=62_000_000),
        name="rim",
    )(x, cot)
    behind = from_behind(tail, 1)
    phases, cot_next, *weights = pl.pallas_call(
        pre_kernel,
        out_shape=(
            shape(frame_count, taps), shape(frame_count, out_width), shape(4 * LANES, LANES), shape(LANES, 2 * LANES),
            shape(2 * LANES, LANES), shape(4 * LANES, taps),
        ),
        in_specs=[VMEM] * 5,
        out_specs=(VMEM,) * 6,
        scratch_shapes=[pltpu.VMEM((length, LANES), F32), pltpu.VMEM((2, frame_count + 8, LANES), F32)],
        compiler_params=pltpu.CompilerParams(vmem_limit_bytes=LIMIT),
        cost_estimate=pl.CostEstimate(flops=10**7, bytes_accessed=6 * 10**6, transcendentals=655360),
        name="pre",
    )(x, cot, w_res, w_proj, down)
    size = 2 * taps * out_width + 3 * channels * hid_width + hid_width * channels
    parts = X * Y * EDGE
    rows = -(-size // (2 * LANES * parts)) * parts
    scale = 1.0 / math.sqrt(clip_count * XC * frame_count * Y * Z)
    mine, other = pl.pallas_call(
        functools.partial(first_kernel, scale),
        out_shape=(shape(rows, LANES), shape(rows, LANES)),
        in_specs=[VMEM] * 8,
        out_specs=(VMEM,) * 2,
        scratch_shapes=[
            pltpu.VMEM((frame_count + EDGE, taps), BF),
            pltpu.VMEM((frame_count + EDGE, 2 * out_width), BF),
            pltpu.VMEM((frame_count + 8, LANES), F32),
            pltpu.VMEM((frame_count + 8, LANES), F32),
            pltpu.VMEM((LANES, 4 * LANES), F32),
            pltpu.VMEM((LANES, 2 * LANES), F32),
        ],
        compiler_params=pltpu.CompilerParams(vmem_limit_bytes=LIMIT),
        cost_estimate=pl.CostEstimate(flops=3 * 10**9, bytes_accessed=8 * 10**6, transcendentals=2 * 10**6),
        name="first",
    )(phases, cot_next, cot, behind, *weights)
    mine, other, (encoded, d_input) = total(mine, other, head, (x, cot, behind), (w_res, w_proj, down))
    grad_res, grad_proj, grad_down = pl.pallas_call(
        last_kernel,
        out_shape=(
            jax.ShapeDtypeStruct((3, hid_width, channels), F32),
            jax.ShapeDtypeStruct((hid_width, channels), F32),
            jax.ShapeDtypeStruct((2 * STRIDE, channels, out_width), F32),
        ),
        in_specs=[VMEM] * 2,
        out_specs=(VMEM,) * 3,
        compiler_params=pltpu.CompilerParams(vmem_limit_bytes=LIMIT),
        name="last",
    )(mine, other)
    return (encoded[None], d_input[None], jnp.transpose(grad_res, (0, 2, 1)), grad_proj, grad_down)


def solution(mesh):
    mesh = Mesh(mesh.devices.reshape(X, CORE, Z, Y), ("x", "core", "z", "y"))
    data = P(("x", "core"), TM, None)
    in_specs = (data, P(), P(), P(), data)
    out_specs = (data, data, P(), P(), P())
    return jax.shard_map(shards, mesh=mesh, in_specs=in_specs, out_specs=out_specs, check_vma=False)
```
